256 devices in a mesh: row: 32 (over z_hi, y, core), col: 8 (over z_lo, x).
Axes of the slice: x: 4, y: 4, z: 8 (z_hi: 4, z_lo: 2; z = z_hi * 2 + z_lo), core: 2. Of those that a mesh axis runs over, the one named last changes fastest.
Arguments:
- y_prev: float32 [256, 65536], P('row', 'col'), may hold values from 0 to 0.1
- t_block: float32 [256, 256], P('row', 'col'), may hold values from 0.001 to 0.01
- c2_panel: float32 [256, 65536], P('row', 'col'), may hold values from 0 to 1
- c1_panel: float32 [8192, 256], P('row', 'col'), may hold values from 0 to 1
- z_prev: float32 [8192, 65536], P('row', 'col'), may hold values from 0 to 650
- row_const: float32 [8192], P('row'), may hold values from 0 to 4
- col_const: float32 [65536], P('col'), may hold values from 0 to 1
- log_row_mass: float32 [8192], P('row'), may hold values from -1 to 1
- log_col_mass: float32 [65536], P('col'), may hold values from -1 to 1
- col_warm: float32 [65536], P('col'), may hold values from -3 to 3
Outputs:
- y_rows: float32 [256, 65536], P('row', 'col')
- row_pot: float32 [8192], P('row')
- col_pot: float32 [65536], P('col')
The draws below stay inside these ranges and needn't reach their ends.
All inputs are finite; a program needn't handle non-finite values.
Results may differ from the reference program's by a relative error of at most 0.0003.
Values sent between devices are 32-bit elements; how exact they have to be, the bound alone decides.
A program may use at most 128 MiB of HBM per device.

```python
import math
import jax
import jax.numpy as jnp
from jax import lax

CELLS2 = 65536
PANEL = 256
SWEEPS = 2
CELLS1 = 8192


def draw_z_prev(key, part):
    base = jax.random.fold_in(key, 4177)
    first = jax.random.fold_in(base, 0)
    third = jax.random.fold_in(base, 2)
    row_level = jax.random.uniform(first, (CELLS1, 1), jnp.float32, 0.0, 500.0)
    noise = jax.random.uniform(third, (CELLS1, CELLS2), jnp.float32, 0.0, 150.0)
    return row_level + noise


def block_levels(key, shape, pieces, smallest, top_value):
    factor_of = 1.0
    for position, blocks in pieces:
        steps = jax.random.uniform(jax.random.fold_in(jax.random.fold_in(key, 6), position), (blocks,), jnp.float32, smallest / len(pieces), top_value / len(pieces))
        factor_of = factor_of * jnp.repeat(jnp.exp(steps), shape[position] // blocks).reshape((-1,) + (1,) * (len(shape) - 1 - position))
    return factor_of


def centred(key, extent, deviation, reach, shards=(), dtype=jnp.bfloat16):
    factor_of = block_levels(key, extent, shards, -0.22, 0.18) if shards else 1.0
    values = jax.random.normal(key, extent, jnp.float32) * deviation * factor_of
    return jnp.minimum(jnp.maximum(values, -reach), reach).astype(dtype)


def setup_inputs(seed: int = 0) -> dict:
    splits = jax.random.split(jax.random.key(seed), 11)
    y_prev = jnp.clip(0.1 * jax.random.uniform(splits[0], (PANEL, CELLS2), jnp.float32) ** block_levels(splits[0], (PANEL, CELLS2), ((0, 32), (1, 8)), -0.2, 0.2), 0.0, 0.1)
    t_block = jnp.clip(jnp.exp(math.log(0.01) - 2.30258502 * jax.random.uniform(splits[1], (PANEL, PANEL), jnp.float32) ** block_levels(splits[1], (PANEL, PANEL), ((0, 32), (1, 8)), -0.2, 0.2)), 0.001, 0.01)
    c2_panel = jnp.clip(1.0 * jax.random.uniform(splits[2], (PANEL, CELLS2), jnp.float32) ** block_levels(splits[2], (PANEL, CELLS2), ((0, 32), (1, 8)), -0.2, 0.2), 0.0, 1.0)
    c1_panel = jnp.clip(1.0 * jax.random.uniform(splits[3], (CELLS1, PANEL), jnp.float32) ** block_levels(splits[3], (CELLS1, PANEL), ((0, 32), (1, 8)), -0.2, 0.2), 0.0, 1.0)
    z_prev = draw_z_prev(jax.random.fold_in(splits[10], 71), 0)
    row_const = jnp.clip(4.0 * jax.random.uniform(splits[5], (CELLS1,), jnp.float32) ** block_levels(splits[5], (CELLS1,), ((0, 32),), -0.2, 0.2), 0.0, 4.0)
    col_const = jnp.clip(1.0 * jax.random.uniform(splits[6], (CELLS2,), jnp.float32) ** block_levels(splits[6], (CELLS2,), ((0, 8),), -0.2, 0.2), 0.0, 1.0)
    log_row_mass = jnp.clip(jax.random.uniform(splits[7], (CELLS1,), jnp.float32, -1.0, 1.0) * block_levels(splits[7], (CELLS1,), ((0, 32),), -0.4, 0.0), -1.0, 1.0)
    log_col_mass = jnp.clip(jax.random.uniform(splits[8], (CELLS2,), jnp.float32, -1.0, 1.0) * block_levels(splits[8], (CELLS2,), ((0, 8),), -0.4, 0.0), -1.0, 1.0)
    col_warm = centred(splits[9], (CELLS2,), 0.5, 3.0, ((0, 8),), jnp.float32)
    return dict(y_prev=y_prev, t_block=t_block, c2_panel=c2_panel, c1_panel=c1_panel, z_prev=z_prev, row_const=row_const, col_const=col_const, log_row_mass=log_row_mass, log_col_mass=log_col_mass, col_warm=col_warm)


epsilon = 5.0


def log_total(scores, axis):
    peak = jnp.max(scores, axis=axis, keepdims=True)
    return jnp.squeeze(peak, axis) + jnp.log(jnp.sum(jnp.exp(scores - peak), axis=axis))


def reference(y_prev, t_block, c2_panel, c1_panel, z_prev, row_const, col_const, log_row_mass, log_col_mass, col_warm):
    highest = lax.Precision.HIGHEST
    y_rows = y_prev + jnp.dot(t_block, c2_panel, precision=highest, preferred_element_type=jnp.float32)
    z_now = z_prev + jnp.dot(c1_panel, y_rows, precision=highest, preferred_element_type=jnp.float32)
    cost = row_const[:, None] + col_const[None, :] - 2.0 * z_now
    col_pot = col_const + col_warm
    row_pot = jnp.zeros_like(row_const)
    for sweep in range(SWEEPS):
        row_pot = epsilon * log_row_mass - epsilon * log_total((col_pot[None, :] - cost) / epsilon, 1)
        col_pot = epsilon * log_col_mass - epsilon * log_total((row_pot[:, None] - cost) / epsilon, 0)
    return y_rows, row_pot, col_pot
```

```python
import jax
import jax.numpy as jnp
from jax import lax
from jax.experimental import pallas as pl
from jax.experimental.pallas import tpu as pltpu
from jax.sharding import PartitionSpec as P

MESH = pl.DeviceIdType.MESH
F32 = jnp.float32
BF16 = jnp.bfloat16
ROWS, COLS = 32, 8
NZ, NY = 4, 4
GROUP = 8
PANEL = 256
HEIGHT = 256
WIDTH = 8192
LANES = 128
TILES = WIDTH // LANES
DEPTH = PANEL // ROWS
EPSILON = 5.0
LOW = -1e30

ORDER = (
    (0, 0, 0), (3, 0, 0), (1, 0, 0), (0, 0, 1),
    (0, 3, 0), (0, 1, 0), (2, 0, 0), (3, 0, 1), (1, 0, 1),
    (0, 3, 1), (0, 1, 1), (3, 3, 0), (1, 3, 0), (3, 1, 0), (1, 1, 0),
    (2, 0, 1), (0, 2, 0), (0, 2, 1),
    (3, 3, 1), (1, 3, 1), (3, 1, 1), (1, 1, 1),
    (2, 3, 0), (2, 1, 0), (3, 2, 0), (1, 2, 0), (3, 2, 1), (1, 2, 1),
    (2, 3, 1), (2, 1, 1), (2, 2, 0), (2, 2, 1),
)


def entry(index, column):
    found = jnp.int32(0)
    for k, item in enumerate(ORDER):
        if item[column]:
            found = jnp.where(index == k, jnp.int32(item[column]), found)
    return found


def three_left(a):
    high = a.astype(BF16)
    low = (a - high.astype(F32)).astype(BF16)
    return jnp.concatenate([high, low, high], axis=1)


def three_right(b):
    high = b.astype(BF16)
    low = (b - high.astype(F32)).astype(BF16)
    return jnp.concatenate([high, high, low], axis=0)


def kernel(
    yp_hbm, t_hbm, c2_hbm, c1_hbm, zp_hbm, rc_ref, cc_ref, lr_ref, lc_ref, cw_ref,
    y_out, row_out, col_out,
    w, ybuf, c2c, ypc, tg, trow, tfull, c1g, left, gcol, run_m, run_s, bcast,
    sx, rx1, rx2, mloc, lcol, part1, part2, u, c1x, c2x, c3x, d1x, d2x, d3x,
    z_sem, t_sems, c1_sems, tf_sems, a_send, a_recv, y_recv, yp_send, ym_send, zz_send, core_send,
    r_send, r_recv, x_send, x_recv,
):
    r, q = lax.axis_index("row"), lax.axis_index("col")
    zh, yy, core = r // GROUP, (r // 2) % NY, r % 2
    g = r % GROUP

    def row_at(dz, dy, c):
        return ((zh + dz) % NZ * NY + (yy + dy) % NY) * 2 + c

    def remote(src, dst, send, recv, row, col):
        return pltpu.make_async_remote_copy(
            src_ref=src, dst_ref=dst, send_sem=send, recv_sem=recv,
            device_id=(row, col), device_id_type=MESH,
        )

    def drain(ref, sem):
        pltpu.make_async_copy(ref, ref, sem).wait()

    def other_rows(do):
        def one(j, carry):
            do((r + j) % ROWS)
            return carry

        lax.fori_loop(1, ROWS, one, 0)

    def other_cols(do):
        def one(j, carry):
            do((q + j) % COLS)
            return carry

        lax.fori_loop(1, COLS, one, 0)

    pltpu.make_async_copy(zp_hbm, w, z_sem).start()

    barrier = pltpu.get_barrier_semaphore()

    def greet(row, col):
        pl.semaphore_signal(barrier, inc=1, device_id=(row, col), device_id_type=MESH)

    other_cols(lambda col: greet(r, col))
    other_rows(lambda row: greet(row, q))
    pl.semaphore_wait(barrier, ROWS + COLS - 2)

    pltpu.make_async_copy(t_hbm, tg.at[q], t_sems.at[1]).start()
    other_cols(lambda col: remote(t_hbm, tg.at[q], t_sems.at[0], t_sems.at[1], r, col).start())

    def scatter(half):
        def columns(row):
            return pl.ds(pl.multiple_of(row * 2 * LANES + half * LANES, LANES), LANES)

        def send(row):
            for src, dst in ((c2_hbm, c2c), (yp_hbm, ypc)):
                remote(
                    src.at[:, columns(row)], dst.at[half, r], a_send.at[half], a_recv.at[half], row, q
                ).start()

        other_rows(send)
        for src, dst in ((c2_hbm, c2c), (yp_hbm, ypc)):
            pltpu.make_async_copy(src.at[:, columns(r)], dst.at[half, r], a_recv.at[half]).start()

    scatter(0)

    drain(tg, t_sems.at[1])
    trow[...] = jnp.concatenate([tg[k] for k in range(COLS)], axis=1)
    mine = pl.ds(pl.multiple_of(r * DEPTH, DEPTH), DEPTH)
    other_rows(lambda row: remote(trow, tfull.at[r], tf_sems.at[0], tf_sems.at[1], row, q).start())
    pltpu.make_async_copy(trow, tfull.at[r], tf_sems.at[1]).start()

    scatter(1)
    pltpu.make_async_copy(c1_hbm, c1g.at[q], c1_sems.at[1]).start()
    other_cols(lambda col: remote(c1_hbm, c1g.at[q], c1_sems.at[0], c1_sems.at[1], r, col).start())

    gcol[...] = cw_ref[...] * (1.0 / EPSILON)
    run_m[...] = jnp.full_like(run_m, LOW)
    run_s[...] = jnp.zeros_like(run_s)

    drain(tfull, tf_sems.at[1])
    t_three = three_left(tfull[...].reshape(PANEL, PANEL))
    left[...] = t_three

    def own_block(half):
        drain(c2c, a_recv.at[half])
        block = jnp.dot(
            left[...], three_right(c2c[half].reshape(PANEL, LANES)), preferred_element_type=F32
        )
        ybuf[r * 2 + half] = ypc[half].reshape(PANEL, LANES) + block

    def block_at(dz, dy, c, half):
        return row_at(dz, dy, c) * 2 + half

    def pass_on(dz, dy, half):
        b = block_at(dz, dy, core, half)
        here = ybuf.at[b]
        up, down = row_at(0, 1, core), row_at(0, NY - 1, core)
        if dy == 0:
            remote(here, here, yp_send, y_recv.at[b], up, q).start()
            remote(here, here, ym_send, y_recv.at[b], down, q).start()
            if dz == 0 or (dz == NZ - 1 and half == 0):
                remote(here, here, zz_send, y_recv.at[b], row_at(1, 0, core), q).start()
            if dz == 0 or (dz == 1 and half == 1):
                remote(here, here, zz_send, y_recv.at[b], row_at(NZ - 1, 0, core), q).start()
        if dy == NY - 1 and half == 0:
            remote(here, here, yp_send, y_recv.at[b], up, q).start()
        if dy == 1 and half == 1:
            remote(here, here, ym_send, y_recv.at[b], down, q).start()
        remote(here, here, core_send, y_recv.at[b], row_at(0, 0, 1 - core), q).start()

    def take(index):
        dy, dz, half = entry(index, 0), entry(index, 1), entry(index, 2)
        first, second = block_at(dz, dy, core, half), block_at(dz, dy, 1 - core, half)
        pltpu.make_async_copy(ybuf.at[second], ybuf.at[second], y_recv.at[second]).wait()
        for b in (first, second):
            y_out[:, pl.ds(pl.multiple_of(b * LANES, LANES), LANES)] = ybuf[b, mine, :]
        both = jnp.concatenate([ybuf[first], ybuf[second]], axis=1)
        product = jnp.dot(left[...], three_right(both), preferred_element_type=F32)
        scores = []
        for side, b in enumerate((first, second)):
            at = pl.ds(pl.multiple_of(b * LANES, LANES), LANES)
            level = 0.4 * (w[:, at] + product[:, side * LANES : (side + 1) * LANES])
            w[:, at] = level
            scores.append(level + gcol[pl.ds(b, 1), :])
        before = run_m[...]
        peak = jnp.maximum(before, jnp.maximum(scores[0], scores[1]))
        total = run_s[...] * jnp.exp(before - peak)
        run_s[...] = total + jnp.exp(scores[0] - peak) + jnp.exp(scores[1] - peak)
        run_m[...] = peak

    own_block(0)

    def event(index, carry):
        for k, (dy, dz, half) in enumerate(ORDER):

            @pl.when(index == k)
            def _():
                b = block_at(dz, dy, core, half)
                if dy or dz:
                    pltpu.make_async_copy(ybuf.at[b], ybuf.at[b], y_recv.at[b]).wait()
                pass_on(dz, dy, half)

        @pl.when(index == 0)
        def _():
            own_block(1)
            drain(c1g, c1_sems.at[1])
            drain(w, z_sem)
            whole = jnp.concatenate([c1g[k] for k in range(COLS)], axis=1)
            left[...] = three_left(whole)

        @pl.when(index > 0)
        def _():
            take(index - 1)

        return carry

    lax.fori_loop(0, len(ORDER), event, 0)
    take(jnp.int32(len(ORDER) - 1))

    def spread(line):
        return jnp.broadcast_to(line, (LANES, HEIGHT)).T

    def swap_cols(value, slot, buffer):
        sx[slot] = value
        buffer[q] = value
        other_cols(
            lambda col: remote(
                sx.at[slot], buffer.at[q], r_send.at[slot], r_recv.at[slot], r, col
            ).start()
        )
        rest = buffer.at[pl.ds(0, COLS - 1)]
        drain(rest, r_recv.at[slot])
        return buffer[...]

    m_t, s_t = run_m[...].T, run_s[...].T
    peak = jnp.max(m_t, axis=0, keepdims=True)
    line = peak + jnp.log(jnp.sum(s_t * jnp.exp(m_t - peak), axis=0, keepdims=True))
    lines = swap_cols(line, 0, rx1)
    peak = jnp.max(lines, axis=0)
    f1 = lr_ref[...] - peak - jnp.log(jnp.sum(jnp.exp(lines - peak[None]), axis=0))
    bcast[...] = spread(f1)

    def column(b, carry):
        at = pl.ds(pl.multiple_of(b * LANES, LANES), LANES)
        scores = w[:, at] + bcast[...]
        top = jnp.max(scores, axis=0, keepdims=True)
        scaled = jnp.exp(scores - top)
        w[:, at] = scaled
        mloc[pl.ds(b, 1), :] = top
        u[pl.ds(b, 1), :] = jnp.sum(scaled, axis=0, keepdims=True)
        return carry

    lax.fori_loop(0, TILES, column, 0, unroll=2)
    lcol[...] = mloc[...] + jnp.log(u[...])

    def swap_rows(source, slot, first, second, third, join):
        def peer(j):
            return zh * GROUP + (g + j) % GROUP

        def group(do):
            def one(j, carry):
                do(peer(j))
                return carry

            lax.fori_loop(1, GROUP, one, 0)

        first[g] = source[pl.ds(pl.multiple_of(g * 8, 8), 8), :]
        group(
            lambda row: remote(
                source.at[pl.ds(pl.multiple_of((row % GROUP) * 8, 8), 8), :],
                first.at[g], x_send.at[slot, 0], x_recv.at[slot, 0], row, q,
            ).start()
        )
        drain(first.at[pl.ds(0, GROUP - 1)], x_recv.at[slot, 0])
        part = join(first[...])
        part1[slot] = part
        second[zh] = part
        for dz in range(1, NZ):
            remote(
                part1.at[slot], second.at[zh], x_send.at[slot, 1], x_recv.at[slot, 1],
                row_at(dz, 0, core), q,
            ).start()
        drain(second.at[pl.ds(0, NZ - 1)], x_recv.at[slot, 1])
        whole = join(second[...])
        part2[slot] = whole
        third[g] = whole
        group(
            lambda row: remote(
                part2.at[slot], third.at[g], x_send.at[slot, 2], x_recv.at[slot, 2], row, q
            ).start()
        )
        drain(third.at[pl.ds(0, GROUP - 1)], x_recv.at[slot, 2])
        return third[...].reshape(TILES, LANES)

    def joined(parts):
        top = jnp.max(parts, axis=0)
        return top + jnp.log(jnp.sum(jnp.exp(parts - top[None]), axis=0))

    g1 = lc_ref[...] - swap_rows(lcol, 0, c1x, c2x, c3x, joined)
    gcol[...] = g1
    u[...] = jnp.exp(g1 + mloc[...])

    def rows(b, total):
        at = pl.ds(pl.multiple_of(b * LANES, LANES), LANES)
        return total + w[:, at] * u[pl.ds(b, 1), :]

    total = lax.fori_loop(0, TILES, rows, jnp.zeros((HEIGHT, LANES), F32), unroll=2)
    run_s[...] = total
    line = jnp.sum(run_s[...].T, axis=0, keepdims=True)
    lines = swap_cols(line, 1, rx2)
    total = jnp.sum(lines, axis=0)
    f2 = lr_ref[...] + f1 - jnp.log(total)
    row_out[...] = rc_ref[...] + EPSILON * f2
    bcast[...] = spread(jnp.exp(lr_ref[...]) / total)

    def columns(b, carry):
        at = pl.ds(pl.multiple_of(b * LANES, LANES), LANES)
        mloc[pl.ds(b, 1), :] = jnp.sum(w[:, at] * bcast[...], axis=0, keepdims=True)
        return carry

    lax.fori_loop(0, TILES, columns, 0, unroll=2)
    lcol2 = mloc
    lcol2[...] = mloc[...] * u[...]
    total = swap_rows(lcol2, 1, d1x, d2x, d3x, lambda parts: jnp.sum(parts, axis=0))
    col_out[...] = cc_ref[...] + EPSILON * (lc_ref[...] + gcol[...] - jnp.log(total))

    drain(tg.at[pl.ds(0, COLS - 1)], t_sems.at[0])
    drain(c1g.at[pl.ds(0, COLS - 1)], c1_sems.at[0])
    drain(tfull.at[pl.ds(0, ROWS - 1)], tf_sems.at[0])
    for half in range(2):
        drain(c2c.at[:, pl.ds(0, ROWS - 1)], a_send.at[half])
    drain(ybuf.at[pl.ds(0, 12)], yp_send)
    drain(ybuf.at[pl.ds(0, 12)], ym_send)
    drain(ybuf.at[pl.ds(0, 6)], zz_send)
    drain(ybuf.at[pl.ds(0, 32)], core_send)
    for slot in range(2):
        drain(rx1.at[pl.ds(0, COLS - 1)], r_send.at[slot])
        drain(c1x.at[pl.ds(0, GROUP - 1)], x_send.at[slot, 0])
        drain(c2x.at[pl.ds(0, NZ - 1)], x_send.at[slot, 1])
        drain(c3x.at[pl.ds(0, GROUP - 1)], x_send.at[slot, 2])


def body(y_prev, t_block, c2_panel, c1_panel, z_prev, row_const, col_const, log_row_mass, log_col_mass, col_warm):
    tall = lambda a: a.reshape(TILES, LANES)
    flat = lambda a: a.reshape(1, HEIGHT)
    hbm = pl.BlockSpec(memory_space=pl.ANY)
    vmem = pl.BlockSpec(memory_space=pltpu.VMEM)
    dma = pltpu.SemaphoreType.DMA
    y_next, row_pot, col_pot = pl.pallas_call(
        kernel,
        out_shape=(
            jax.ShapeDtypeStruct((DEPTH, WIDTH), F32),
            jax.ShapeDtypeStruct((1, HEIGHT), F32),
            jax.ShapeDtypeStruct((TILES, LANES), F32),
        ),
        in_specs=[hbm] * 5 + [vmem] * 5,
        out_specs=(vmem, vmem, vmem),
        scratch_shapes=[
            pltpu.VMEM((HEIGHT, WIDTH), F32),
            pltpu.VMEM((TILES, PANEL, LANES), F32),
            pltpu.VMEM((2, ROWS, DEPTH, LANES), F32),
            pltpu.VMEM((2, ROWS, DEPTH, LANES), F32),
            pltpu.VMEM((COLS, DEPTH, PANEL // COLS), F32),
            pltpu.VMEM((DEPTH, PANEL), F32),
            pltpu.VMEM((ROWS, DEPTH, PANEL), F32),
            pltpu.VMEM((COLS, HEIGHT, PANEL // COLS), F32),
            pltpu.VMEM((HEIGHT, 3 * PANEL), BF16),
            pltpu.VMEM((TILES, LANES), F32),
            pltpu.VMEM((HEIGHT, LANES), F32),
            pltpu.VMEM((HEIGHT, LANES), F32),
            pltpu.VMEM((HEIGHT, LANES), F32),
            pltpu.VMEM((2, 1, HEIGHT), F32),
            pltpu.VMEM((COLS, 1, HEIGHT), F32),
            pltpu.VMEM((COLS, 1, HEIGHT), F32),
            pltpu.VMEM((TILES, LANES), F32),
            pltpu.VMEM((TILES, LANES), F32),
            pltpu.VMEM((2, 8, LANES), F32),
            pltpu.VMEM((2, 8, LANES), F32),
            pltpu.VMEM((TILES, LANES), F32),
            pltpu.VMEM((GROUP, 8, LANES), F32),
            pltpu.VMEM((NZ, 8, LANES), F32),
            pltpu.VMEM((GROUP, 8, LANES), F32),
            pltpu.VMEM((GROUP, 8, LANES), F32),
            pltpu.VMEM((NZ, 8, LANES), F32),
            pltpu.VMEM((GROUP, 8, LANES), F32),
            dma,
            dma((2,)),
            dma((2,)),
            dma((2,)),
            dma((2,)),
            dma((2,)),
            dma((TILES,)),
            dma,
            dma,
            dma,
            dma,
            dma((2,)),
            dma((2,)),
            dma((2, 3)),
            dma((2, 3)),
        ],
        compiler_params=pltpu.CompilerParams(
            collective_id=0, has_side_effects=True, vmem_limit_bytes=56 * 1024 * 1024
        ),
        name="step",
    )(
        y_prev, t_block, c2_panel, c1_panel, z_prev, flat(row_const), tall(col_const),
        flat(log_row_mass), tall(log_col_mass), tall(col_warm),
    )
    return y_next, row_pot.reshape(HEIGHT), col_pot.reshape(WIDTH)


def solution(mesh):
    block = P("row", "col")
    return jax.shard_map(
        body,
        mesh=mesh,
        in_specs=(block,) * 5 + (P("row"), P("col"), P("row"), P("col"), P("col")),
        out_specs=(block, P("row"), P("col")),
        check_vma=False,
    )
```

```python
import jax
import jax.numpy as jnp
from jax import lax
from jax.experimental import pallas as pl
from jax.experimental.pallas import tpu as pltpu
from jax.sharding import PartitionSpec as P

MESH = pl.DeviceIdType.MESH
F32 = jnp.float32
BF16 = jnp.bfloat16
ROWS, COLS = 32, 8
NZ, NY = 4, 4
GROUP = 8
PANEL = 256
HEIGHT = 256
WIDTH = 8192
LANES = 128
TILES = WIDTH // LANES
DEPTH = PANEL // ROWS
T_COLS = PANEL // COLS
EPSILON = 5.0
LOW = -1e30

ORDER = (
    (0, 0, 0), (3, 0, 0), (1, 0, 0), (0, 0, 1),
    (0, 3, 0), (0, 1, 0), (2, 0, 0), (3, 0, 1), (1, 0, 1),
    (0, 3, 1), (0, 1, 1), (3, 3, 0), (1, 3, 0), (3, 1, 0), (1, 1, 0),
    (2, 0, 1), (0, 2, 0), (0, 2, 1),
    (3, 3, 1), (1, 3, 1), (3, 1, 1), (1, 1, 1),
    (2, 3, 0), (2, 1, 0), (3, 2, 0), (1, 2, 0), (3, 2, 1), (1, 2, 1),
    (2, 3, 1), (2, 1, 1), (2, 2, 0), (2, 2, 1),
)


def entry(index, column):
    found = jnp.int32(0)
    for k, item in enumerate(ORDER):
        if item[column]:
            found = jnp.where(index == k, jnp.int32(item[column]), found)
    return found


def three_left(a):
    high = a.astype(BF16)
    low = (a - high.astype(F32)).astype(BF16)
    return jnp.concatenate([high, low, high], axis=1)


def three_right(b):
    high = b.astype(BF16)
    low = (b - high.astype(F32)).astype(BF16)
    return jnp.concatenate([high, high, low], axis=0)


def kernel(
    yp_hbm, t_ref, c2_hbm, c1_hbm, zp_hbm, rc_ref, cc_ref, lr_ref, lc_ref, cw_ref,
    y_out, row_out, col_out,
    w, ybuf, c2c, ypc, tpad, tg, trow, tfull, c1g, left, gcol, run_m, run_s, bcast,
    sx, rx1, rx2, mloc, lcol, part1, part2, u, c1x, c2x, c3x, d1x, d2x, d3x,
    z_sem, t_sems, c1_sems, tf_sems, a_send, a_recv, y_recv, yp_send, ym_send, zz_send, core_send,
    r_send, r_recv, x_send, x_recv,
):
    r, q = lax.axis_index("row"), lax.axis_index("col")
    zh, yy, core = r // GROUP, (r // 2) % NY, r % 2
    g = r % GROUP

    def row_at(dz, dy, c):
        return ((zh + dz) % NZ * NY + (yy + dy) % NY) * 2 + c

    def remote(src, dst, send, recv, row, col):
        return pltpu.make_async_remote_copy(
            src_ref=src, dst_ref=dst, send_sem=send, recv_sem=recv,
            device_id=(row, col), device_id_type=MESH,
        )

    def drain(ref, sem):
        pltpu.make_async_copy(ref, ref, sem).wait()

    def other_rows(do):
        def one(j, carry):
            do((r + j) % ROWS)
            return carry

        lax.fori_loop(1, ROWS, one, 0)

    def other_cols(do):
        def one(j, carry):
            do((q + j) % COLS)
            return carry

        lax.fori_loop(1, COLS, one, 0)

    pltpu.make_async_copy(zp_hbm, w, z_sem).start()

    tpad[...] = jnp.concatenate([t_ref[...]] * (LANES // T_COLS), axis=1)

    barrier = pltpu.get_barrier_semaphore()

    def greet(row, col):
        pl.semaphore_signal(barrier, inc=1, device_id=(row, col), device_id_type=MESH)

    other_cols(lambda col: greet(r, col))
    other_rows(lambda row: greet(row, q))
    pl.semaphore_wait(barrier, ROWS + COLS - 2)

    other_cols(lambda col: remote(tpad, tg.at[q], t_sems.at[0], t_sems.at[1], r, col).start())
    pltpu.make_async_copy(tpad, tg.at[q], t_sems.at[1]).start()

    def scatter(half):
        def columns(row):
            return pl.ds(pl.multiple_of(row * 2 * LANES + half * LANES, LANES), LANES)

        def send(row):
            for src, dst in ((c2_hbm, c2c), (yp_hbm, ypc)):
                remote(
                    src.at[:, columns(row)], dst.at[half, r], a_send.at[half], a_recv.at[half], row, q
                ).start()

        other_rows(send)
        for src, dst in ((c2_hbm, c2c), (yp_hbm, ypc)):
            pltpu.make_async_copy(src.at[:, columns(r)], dst.at[half, r], a_recv.at[half]).start()

    scatter(0)

    drain(tg, t_sems.at[1])
    trow[...] = jnp.concatenate([tg[k][:, :T_COLS] for k in range(COLS)], axis=1)
    mine = pl.ds(pl.multiple_of(r * DEPTH, DEPTH), DEPTH)
    other_rows(lambda row: remote(trow, tfull.at[r], tf_sems.at[0], tf_sems.at[1], row, q).start())
    pltpu.make_async_copy(trow, tfull.at[r], tf_sems.at[1]).start()

    scatter(1)
    pltpu.make_async_copy(c1_hbm, c1g.at[q], c1_sems.at[1]).start()
    other_cols(lambda col: remote(c1_hbm, c1g.at[q], c1_sems.at[0], c1_sems.at[1], r, col).start())

    gcol[...] = cw_ref[...] * (1.0 / EPSILON)
    run_m[...] = jnp.full_like(run_m, LOW)
    run_s[...] = jnp.zeros_like(run_s)

    drain(tfull, tf_sems.at[1])
    t_three = three_left(tfull[...].reshape(PANEL, PANEL))
    left[...] = t_three

    def own_block(half):
        drain(c2c, a_recv.at[half])
        block = jnp.dot(
            left[...], three_right(c2c[half].reshape(PANEL, LANES)), preferred_element_type=F32
        )
        ybuf[r * 2 + half] = ypc[half].reshape(PANEL, LANES) + block

    def block_at(dz, dy, c, half):
        return row_at(dz, dy, c) * 2 + half

    def pass_on(dz, dy, half):
        b = block_at(dz, dy, core, half)
        here = ybuf.at[b]
        up, down = row_at(0, 1, core), row_at(0, NY - 1, core)
        if dy == 0:
            remote(here, here, yp_send, y_recv.at[b], up, q).start()
            remote(here, here, ym_send, y_recv.at[b], down, q).start()
            if dz == 0 or (dz == NZ - 1 and half == 0):
                remote(here, here, zz_send, y_recv.at[b], row_at(1, 0, core), q).start()
            if dz == 0 or (dz == 1 and half == 1):
                remote(here, here, zz_send, y_recv.at[b], row_at(NZ - 1, 0, core), q).start()
        if dy == NY - 1 and half == 0:
            remote(here, here, yp_send, y_recv.at[b], up, q).start()
        if dy == 1 and half == 1:
            remote(here, here, ym_send, y_recv.at[b], down, q).start()
        remote(here, here, core_send, y_recv.at[b], row_at(0, 0, 1 - core), q).start()

    def take(index):
        dy, dz, half = entry(index, 0), entry(index, 1), entry(index, 2)
        first, second = block_at(dz, dy, core, half), block_at(dz, dy, 1 - core, half)
        pltpu.make_async_copy(ybuf.at[second], ybuf.at[second], y_recv.at[second]).wait()
        for b in (first, second):
            y_out[:, pl.ds(pl.multiple_of(b * LANES, LANES), LANES)] = ybuf[b, mine, :]
        both = jnp.concatenate([ybuf[first], ybuf[second]], axis=1)
        product = jnp.dot(left[...], three_right(both), preferred_element_type=F32)
        scores = []
        for side, b in enumerate((first, second)):
            at = pl.ds(pl.multiple_of(b * LANES, LANES), LANES)
            level = 0.4 * (w[:, at] + product[:, side * LANES : (side + 1) * LANES])
            w[:, at] = level
            scores.append(level + gcol[pl.ds(b, 1), :])
        before = run_m[...]
        peak = jnp.maximum(before, jnp.maximum(scores[0], scores[1]))
        total = run_s[...] * jnp.exp(before - peak)
        run_s[...] = total + jnp.exp(scores[0] - peak) + jnp.exp(scores[1] - peak)
        run_m[...] = peak

    own_block(0)

    def event(index, carry):
        for k, (dy, dz, half) in enumerate(ORDER):

            @pl.when(index == k)
            def _():
                b = block_at(dz, dy, core, half)
                if dy or dz:
                    pltpu.make_async_copy(ybuf.at[b], ybuf.at[b], y_recv.at[b]).wait()
                pass_on(dz, dy, half)

        @pl.when(index == 0)
        def _():
            own_block(1)
            drain(c1g, c1_sems.at[1])
            drain(w, z_sem)
            left[...] = three_left(c1g[...].reshape(PANEL, HEIGHT).T)

        @pl.when(index > 0)
        def _():
            take(index - 1)

        return carry

    lax.fori_loop(0, len(ORDER), event, 0)
    take(jnp.int32(len(ORDER) - 1))

    def spread(line):
        return jnp.broadcast_to(line, (LANES, HEIGHT)).T

    def swap_cols(value, slot, buffer):
        sx[slot] = value
        buffer[q] = value
        other_cols(
            lambda col: remote(
                sx.at[slot], buffer.at[q], r_send.at[slot], r_recv.at[slot], r, col
            ).start()
        )
        rest = buffer.at[pl.ds(0, COLS - 1)]
        drain(rest, r_recv.at[slot])
        return buffer[...]

    m_t, s_t = run_m[...].T, run_s[...].T
    peak = jnp.max(m_t, axis=0, keepdims=True)
    line = peak + jnp.log(jnp.sum(s_t * jnp.exp(m_t - peak), axis=0, keepdims=True))
    lines = swap_cols(line, 0, rx1)
    peak = jnp.max(lines, axis=0)
    f1 = lr_ref[...] - peak - jnp.log(jnp.sum(jnp.exp(lines - peak[None]), axis=0))
    bcast[...] = spread(f1)

    def column(b, carry):
        at = pl.ds(pl.multiple_of(b * LANES, LANES), LANES)
        scores = w[:, at] + bcast[...]
        top = jnp.max(scores, axis=0, keepdims=True)
        scaled = jnp.exp(scores - top)
        w[:, at] = scaled
        mloc[pl.ds(b, 1), :] = top
        u[pl.ds(b, 1), :] = jnp.sum(scaled, axis=0, keepdims=True)
        return carry

    lax.fori_loop(0, TILES, column, 0, unroll=2)
    lcol[...] = mloc[...] + jnp.log(u[...])

    def swap_rows(source, slot, first, second, third, join):
        def peer(j):
            return zh * GROUP + (g + j) % GROUP

        def group(do):
            def one(j, carry):
                do(peer(j))
                return carry

            lax.fori_loop(1, GROUP, one, 0)

        first[g] = source[pl.ds(pl.multiple_of(g * 8, 8), 8), :]
        group(
            lambda row: remote(
                source.at[pl.ds(pl.multiple_of((row % GROUP) * 8, 8), 8), :],
                first.at[g], x_send.at[slot, 0], x_recv.at[slot, 0], row, q,
            ).start()
        )
        drain(first.at[pl.ds(0, GROUP - 1)], x_recv.at[slot, 0])
        part = join(first[...])
        part1[slot] = part
        second[zh] = part
        for dz in range(1, NZ):
            remote(
                part1.at[slot], second.at[zh], x_send.at[slot, 1], x_recv.at[slot, 1],
                row_at(dz, 0, core), q,
            ).start()
        drain(second.at[pl.ds(0, NZ - 1)], x_recv.at[slot, 1])
        whole = join(second[...])
        part2[slot] = whole
        third[g] = whole
        group(
            lambda row: remote(
                part2.at[slot], third.at[g], x_send.at[slot, 2], x_recv.at[slot, 2], row, q
            ).start()
        )
        drain(third.at[pl.ds(0, GROUP - 1)], x_recv.at[slot, 2])
        return third[...].reshape(TILES, LANES)

    def joined(parts):
        top = jnp.max(parts, axis=0)
        return top + jnp.log(jnp.sum(jnp.exp(parts - top[None]), axis=0))

    g1 = lc_ref[...] - swap_rows(lcol, 0, c1x, c2x, c3x, joined)
    gcol[...] = g1
    u[...] = jnp.exp(g1 + mloc[...])

    def rows(b, total):
        at = pl.ds(pl.multiple_of(b * LANES, LANES), LANES)
        return total + w[:, at] * u[pl.ds(b, 1), :]

    total = lax.fori_loop(0, TILES, rows, jnp.zeros((HEIGHT, LANES), F32), unroll=2)
    run_s[...] = total
    line = jnp.sum(run_s[...].T, axis=0, keepdims=True)
    lines = swap_cols(line, 1, rx2)
    total = jnp.sum(lines, axis=0)
    f2 = lr_ref[...] + f1 - jnp.log(total)
    row_out[...] = rc_ref[...] + EPSILON * f2
    bcast[...] = spread(jnp.exp(lr_ref[...]) / total)

    def columns(b, carry):
        at = pl.ds(pl.multiple_of(b * LANES, LANES), LANES)
        mloc[pl.ds(b, 1), :] = jnp.sum(w[:, at] * bcast[...], axis=0, keepdims=True)
        return carry

    lax.fori_loop(0, TILES, columns, 0, unroll=2)
    lcol2 = mloc
    lcol2[...] = mloc[...] * u[...]
    total = swap_rows(lcol2, 1, d1x, d2x, d3x, lambda parts: jnp.sum(parts, axis=0))
    col_out[...] = cc_ref[...] + EPSILON * (lc_ref[...] + gcol[...] - jnp.log(total))

    drain(tg.at[pl.ds(0, COLS - 1)], t_sems.at[0])
    drain(c1g.at[pl.ds(0, COLS - 1)], c1_sems.at[0])
    drain(tfull.at[pl.ds(0, ROWS - 1)], tf_sems.at[0])
    for half in range(2):
        drain(c2c.at[:, pl.ds(0, ROWS - 1)], a_send.at[half])
    drain(ybuf.at[pl.ds(0, 12)], yp_send)
    drain(ybuf.at[pl.ds(0, 12)], ym_send)
    drain(ybuf.at[pl.ds(0, 6)], zz_send)
    drain(ybuf.at[pl.ds(0, 32)], core_send)
    for slot in range(2):
        drain(rx1.at[pl.ds(0, COLS - 1)], r_send.at[slot])
        drain(c1x.at[pl.ds(0, GROUP - 1)], x_send.at[slot, 0])
        drain(c2x.at[pl.ds(0, NZ - 1)], x_send.at[slot, 1])
        drain(c3x.at[pl.ds(0, GROUP - 1)], x_send.at[slot, 2])


def handed_on(*refs):
    for source, target in zip(refs[:3], refs[3:]):
        target[...] = source[...]


def body(y_prev, t_block, c2_panel, c1_panel, z_prev, row_const, col_const, log_row_mass, log_col_mass, col_warm):
    tall = lambda a: a.reshape(TILES, LANES)
    flat = lambda a: a.reshape(1, HEIGHT)
    hbm = pl.BlockSpec(memory_space=pl.ANY)
    vmem = pl.BlockSpec(memory_space=pltpu.VMEM)
    dma = pltpu.SemaphoreType.DMA
    y_next, row_pot, col_pot = pl.pallas_call(
        kernel,
        out_shape=(
            jax.ShapeDtypeStruct((DEPTH, WIDTH), F32),
            jax.ShapeDtypeStruct((1, HEIGHT), F32),
            jax.ShapeDtypeStruct((TILES, LANES), F32),
        ),
        in_specs=[hbm, vmem, hbm, hbm, hbm] + [vmem] * 5,
        out_specs=(vmem, vmem, vmem),
        scratch_shapes=[
            pltpu.VMEM((HEIGHT, WIDTH), F32),
            pltpu.VMEM((TILES, PANEL, LANES), F32),
            pltpu.VMEM((2, ROWS, DEPTH, LANES), F32),
            pltpu.VMEM((2, ROWS, DEPTH, LANES), F32),
            pltpu.VMEM((DEPTH, LANES), F32),
            pltpu.VMEM((COLS, DEPTH, LANES), F32),
            pltpu.VMEM((DEPTH, PANEL), F32),
            pltpu.VMEM((ROWS, DEPTH, PANEL), F32),
            pltpu.VMEM((COLS, T_COLS, HEIGHT), F32),
            pltpu.VMEM((HEIGHT, 3 * PANEL), BF16),
            pltpu.VMEM((TILES, LANES), F32),
            pltpu.VMEM((HEIGHT, LANES), F32),
            pltpu.VMEM((HEIGHT, LANES), F32),
            pltpu.VMEM((HEIGHT, LANES), F32),
            pltpu.VMEM((2, 1, HEIGHT), F32),
            pltpu.VMEM((COLS, 1, HEIGHT), F32),
            pltpu.VMEM((COLS, 1, HEIGHT), F32),
            pltpu.VMEM((TILES, LANES), F32),
            pltpu.VMEM((TILES, LANES), F32),
            pltpu.VMEM((2, 8, LANES), F32),
            pltpu.VMEM((2, 8, LANES), F32),
            pltpu.VMEM((TILES, LANES), F32),
            pltpu.VMEM((GROUP, 8, LANES), F32),
            pltpu.VMEM((NZ, 8, LANES), F32),
            pltpu.VMEM((GROUP, 8, LANES), F32),
            pltpu.VMEM((GROUP, 8, LANES), F32),
            pltpu.VMEM((NZ, 8, LANES), F32),
            pltpu.VMEM((GROUP, 8, LANES), F32),
            dma,
            dma((2,)),
            dma((2,)),
            dma((2,)),
            dma((2,)),
            dma((2,)),
            dma((TILES,)),
            dma,
            dma,
            dma,
            dma,
            dma((2,)),
            dma((2,)),
            dma((2, 3)),
            dma((2, 3)),
        ],
        compiler_params=pltpu.CompilerParams(
            collective_id=0, has_side_effects=True, vmem_limit_bytes=56 * 1024 * 1024
        ),
        name="step",
    )(
        y_prev, t_block, c2_panel, c1_panel.T, z_prev, flat(row_const), tall(col_const),
        flat(log_row_mass), tall(log_col_mass), tall(col_warm),
    )
    y_next, row_pot, col_pot = pl.pallas_call(
        handed_on,
        out_shape=(
            jax.ShapeDtypeStruct((DEPTH, WIDTH), F32),
            jax.ShapeDtypeStruct((1, HEIGHT), F32),
            jax.ShapeDtypeStruct((TILES, LANES), F32),
        ),
        in_specs=[vmem] * 3,
        out_specs=(vmem, vmem, vmem),
        name="results",
    )(y_next, row_pot, col_pot)
    return y_next, row_pot.reshape(HEIGHT), col_pot.reshape(WIDTH)


def solution(mesh):
    block = P("row", "col")
    return jax.shard_map(
        body,
        mesh=mesh,
        in_specs=(block,) * 5 + (P("row"), P("col"), P("row"), P("col"), P("col")),
        out_specs=(block, P("row"), P("col")),
        check_vma=False,
    )
```

```python
import jax
import jax.numpy as jnp
from jax import lax
from jax.experimental import pallas as pl
from jax.experimental.pallas import tpu as pltpu
from jax.sharding import PartitionSpec as P

MESH = pl.DeviceIdType.MESH
F32 = jnp.float32
BF16 = jnp.bfloat16
ROWS, COLS = 32, 8
NZ, NY = 4, 4
GROUP = 8
CHIPS = NZ * NY
PANEL = 256
HEIGHT = 256
WIDTH = 8192
LANES = 128
TILES = WIDTH // LANES
DEPTH = PANEL // ROWS
T_COLS = PANEL // COLS
EPSILON = 5.0
LOW = -1e30
BEHIND = 1

ORDER = (
    (0, 0, 0), (3, 0, 0), (1, 0, 0), (0, 0, 1),
    (0, 3, 0), (0, 1, 0), (2, 0, 0), (3, 0, 1), (1, 0, 1),
    (0, 3, 1), (0, 1, 1), (3, 3, 0), (1, 3, 0), (3, 1, 0), (1, 1, 0),
    (2, 0, 1), (0, 2, 0), (0, 2, 1),
    (3, 3, 1), (1, 3, 1), (3, 1, 1), (1, 1, 1),
    (2, 3, 0), (2, 1, 0), (3, 2, 0), (1, 2, 0), (3, 2, 1), (1, 2, 1),
    (2, 3, 1), (2, 1, 1), (2, 2, 0), (2, 2, 1),
)


def entry(index):
    found = jnp.int32(0)
    for k, (dy, dz, half) in enumerate(ORDER):
        if k:
            found = jnp.where(index == k, jnp.int32(dy * 8 + dz * 2 + half), found)
    return found


def three_left(a):
    high = a.astype(BF16)
    low = (a - high.astype(F32)).astype(BF16)
    return jnp.concatenate([high, low, high], axis=1)


def three_right(b):
    high = b.astype(BF16)
    low = (b - high.astype(F32)).astype(BF16)
    return jnp.concatenate([high, high, low], axis=0)


def kernel(
    yp_hbm, t_ref, c2_hbm, c1_hbm, zp_hbm, rc_ref, cc_ref, lr_ref, lc_ref, cw_ref,
    y_out, row_out, col_out,
    w, ybuf, c2c, ypc, tpad, tg, trow, tfull, c1g, left, gcol, run_m, run_s, bcast,
    sx, rx1, rx2, mloc, lcol, lcol2, part1, part2, u, c1x, c2x, c3x, d1x, d2x, d3x,
    z_sem, t_sems, c1_sems, tf_sems, a_send, a_recv, y_recv, yp_send, ym_send, zz_send, core_send,
    r_send, r_recv, x_send, x_recv, p_recv, q_recv,
):
    r, q = lax.axis_index("row"), lax.axis_index("col")
    zh, yy, core = r // GROUP, (r // 2) % NY, r % 2
    g = r % GROUP

    def row_at(dz, dy, c):
        return ((zh + dz) % NZ * NY + (yy + dy) % NY) * 2 + c

    def remote(src, dst, send, recv, row, col):
        return pltpu.make_async_remote_copy(
            src_ref=src, dst_ref=dst, send_sem=send, recv_sem=recv,
            device_id=(row, col), device_id_type=MESH,
        )

    def drain(ref, sem):
        pltpu.make_async_copy(ref, ref, sem).wait()

    def other_rows(do):
        def one(j, carry):
            do((r + j) % ROWS)
            return carry

        lax.fori_loop(1, ROWS, one, 0)

    def other_cols(do):
        def one(j, carry):
            do((q + j) % COLS)
            return carry

        lax.fori_loop(1, COLS, one, 0)

    pltpu.make_async_copy(zp_hbm, w, z_sem).start()

    tpad[...] = jnp.concatenate([t_ref[...]] * (LANES // T_COLS), axis=1)

    barrier = pltpu.get_barrier_semaphore()

    def greet(row, col):
        pl.semaphore_signal(barrier, inc=1, device_id=(row, col), device_id_type=MESH)

    other_cols(lambda col: greet(r, col))
    other_rows(lambda row: greet(row, q))
    pl.semaphore_wait(barrier, ROWS + COLS - 2)

    other_cols(lambda col: remote(tpad, tg.at[q], t_sems.at[0], t_sems.at[1], r, col).start())
    pltpu.make_async_copy(tpad, tg.at[q], t_sems.at[1]).start()

    def scatter(half):
        def columns(row):
            return pl.ds(pl.multiple_of(row * 2 * LANES + half * LANES, LANES), LANES)

        def send(row):
            for src, dst in ((c2_hbm, c2c), (yp_hbm, ypc)):
                remote(
                    src.at[:, columns(row)], dst.at[half, r], a_send.at[half], a_recv.at[half], row, q
                ).start()

        other_rows(send)
        for src, dst in ((c2_hbm, c2c), (yp_hbm, ypc)):
            pltpu.make_async_copy(src.at[:, columns(r)], dst.at[half, r], a_recv.at[half]).start()

    scatter(0)

    drain(tg, t_sems.at[1])
    trow[...] = jnp.concatenate([tg[k][:, :T_COLS] for k in range(COLS)], axis=1)
    mine = pl.ds(pl.multiple_of(r * DEPTH, DEPTH), DEPTH)
    pltpu.make_async_copy(trow, tfull.at[r // 2, core], tf_sems.at[1]).start()

    def to_chip(j, carry):
        row = (r // 2 + j) % CHIPS * 2 + core
        remote(trow, tfull.at[r // 2, core], tf_sems.at[0], tf_sems.at[1], row, q).start()
        return carry

    lax.fori_loop(1, CHIPS, to_chip, 0)

    scatter(1)
    pltpu.make_async_copy(c1_hbm, c1g.at[q], c1_sems.at[1]).start()
    other_cols(lambda col: remote(c1_hbm, c1g.at[q], c1_sems.at[0], c1_sems.at[1], r, col).start())

    gcol[...] = cw_ref[...] * (1.0 / EPSILON)
    run_m[...] = jnp.full_like(run_m, LOW)
    run_s[...] = jnp.zeros_like(run_s)

    drain(tfull.at[:, core], tf_sems.at[1])
    half_t = tfull.at[:, core]
    remote(half_t, half_t, tf_sems.at[2], tf_sems.at[3], row_at(0, 0, 1 - core), q).start()
    drain(tfull.at[:, 1 - core], tf_sems.at[3])
    t_three = three_left(tfull[...].reshape(PANEL, PANEL))
    left[...] = t_three

    def own_block(half):
        drain(c2c, a_recv.at[half])
        block = jnp.dot(
            left[...], three_right(c2c[half].reshape(PANEL, LANES)), preferred_element_type=F32
        )
        ybuf[r * 2 + half] = ypc[half].reshape(PANEL, LANES) + block

    def block_at(dz, dy, c, half):
        return row_at(dz, dy, c) * 2 + half

    def pass_on(dz, dy, half):
        b = block_at(dz, dy, core, half)
        here = ybuf.at[b]
        near, first = dy == 0, half == 0
        start = near & (dz == 0)

        def hand(condition, send, row):
            @pl.when(condition)
            def _():
                remote(here, here, send, y_recv.at[b], row, q).start()

        @pl.when(~start)
        def _():
            pltpu.make_async_copy(here, here, y_recv.at[b]).wait()

        hand(near | ((dy == NY - 1) & first), yp_send, row_at(0, 1, core))
        hand(near | ((dy == 1) & ~first), ym_send, row_at(0, NY - 1, core))
        hand(start | (near & (dz == NZ - 1) & first), zz_send, row_at(1, 0, core))
        hand(start | (near & (dz == 1) & ~first), zz_send, row_at(NZ - 1, 0, core))
        remote(here, here, core_send, y_recv.at[b], row_at(0, 0, 1 - core), q).start()

    def parted(code):
        return code // 8, code // 2 % 4, code % 2

    def take(code):
        dy, dz, half = parted(code)
        first, second = block_at(dz, dy, core, half), block_at(dz, dy, 1 - core, half)
        pltpu.make_async_copy(ybuf.at[second], ybuf.at[second], y_recv.at[second]).wait()
        for b in (first, second):
            y_out[:, pl.ds(pl.multiple_of(b * LANES, LANES), LANES)] = ybuf[b, mine, :]
        both = jnp.concatenate([ybuf[first], ybuf[second]], axis=1)
        product = jnp.dot(left[...], three_right(both), preferred_element_type=F32)
        scores = []
        for side, b in enumerate((first, second)):
            at = pl.ds(pl.multiple_of(b * LANES, LANES), LANES)
            level = 0.4 * (w[:, at] + product[:, side * LANES : (side + 1) * LANES])
            w[:, at] = level
            scores.append(level + gcol[pl.ds(b, 1), :])
        before = run_m[...]
        peak = jnp.maximum(before, jnp.maximum(scores[0], scores[1]))
        total = run_s[...] * jnp.exp(before - peak)
        run_s[...] = total + jnp.exp(scores[0] - peak) + jnp.exp(scores[1] - peak)
        run_m[...] = peak

    own_block(0)

    def event(index, before):
        code = entry(index)
        dy, dz, half = parted(code)

        @pl.when(index < len(ORDER))
        def _():
            pass_on(dz, dy, half)

        @pl.when(index == 0)
        def _():
            own_block(1)
            drain(c1g, c1_sems.at[1])
            drain(w, z_sem)
            left[...] = three_left(c1g[...].reshape(PANEL, HEIGHT).T)

        @pl.when(index >= BEHIND)
        def _():
            take(before[-1])

        return (code, *before[:-1])

    lax.fori_loop(0, len(ORDER) + BEHIND, event, (jnp.int32(0),) * BEHIND)

    def spread(line):
        return jnp.broadcast_to(line, (LANES, HEIGHT)).T

    def swap_cols(value, slot, buffer):
        sx[slot] = value
        buffer[q] = value
        other_cols(
            lambda col: remote(
                sx.at[slot], buffer.at[q], r_send.at[slot], r_recv.at[slot], r, col
            ).start()
        )
        rest = buffer.at[pl.ds(0, COLS - 1)]
        drain(rest, r_recv.at[slot])
        return buffer[...]

    m_t, s_t = run_m[...].T, run_s[...].T
    peak = jnp.max(m_t, axis=0, keepdims=True)
    line = peak + jnp.log(jnp.sum(s_t * jnp.exp(m_t - peak), axis=0, keepdims=True))
    lines = swap_cols(line, 0, rx1)
    peak = jnp.max(lines, axis=0)
    f1 = lr_ref[...] - peak - jnp.log(jnp.sum(jnp.exp(lines - peak[None]), axis=0))
    bcast[...] = spread(f1)

    def tile(b):
        return pl.ds(pl.multiple_of(b * LANES, LANES), LANES)

    def part_at(j):
        pair = j // 2
        dy = jnp.where(pair == 0, 2, jnp.where(pair == 1, 1, jnp.where(pair == 2, 3, 0)))
        return (yy + dy) % NY * 2 + (core + 1 + j) % 2

    def column_parts(work, source, slot, first):
        def one(j, carry):
            part = part_at(j)
            at = pl.ds(pl.multiple_of(part * 8, 8), 8)
            work(part * 8, at)

            @pl.when(j < GROUP - 1)
            def _():
                remote(
                    source.at[at, :], first.at[g], x_send.at[slot, 0], x_recv.at[slot, 0],
                    zh * GROUP + part, q,
                ).start()

            return carry

        lax.fori_loop(0, GROUP, one, 0)

    def first_columns(b, at):
        tops, sums = [], []
        for k in range(8):
            scores = w[:, tile(b + k)] + bcast[...]
            top = jnp.max(scores, axis=0, keepdims=True)
            scaled = jnp.exp(scores - top)
            w[:, tile(b + k)] = scaled
            tops.append(top)
            sums.append(jnp.sum(scaled, axis=0, keepdims=True))
        top = jnp.concatenate(tops, axis=0)
        mloc[at, :] = top
        lcol[at, :] = top + jnp.log(jnp.concatenate(sums, axis=0))

    column_parts(first_columns, lcol, 0, c1x)

    def join_rows(source, slot, first, second, third, join, p_recv):
        first[g] = source[pl.ds(pl.multiple_of(g * 8, 8), 8), :]
        drain(first.at[pl.ds(0, GROUP - 1)], x_recv.at[slot, 0])
        part = join(first[...])
        part1[slot] = part
        for dz in (2, 1, 3):
            remote(
                part1.at[slot], second.at[zh], x_send.at[slot, 1], x_recv.at[slot, 1],
                row_at(dz, 0, core), q,
            ).start()
        second[zh] = part
        drain(second.at[pl.ds(0, NZ - 1)], x_recv.at[slot, 1])
        whole = join(second[...])
        part2[slot] = whole

        def one(j, carry):
            row = zh * GROUP + part_at(j)
            remote(part2.at[slot], third.at[g], x_send.at[slot, 2], p_recv.at[g], row, q).start()
            return carry

        lax.fori_loop(0, GROUP - 1, one, 0)
        third[g] = whole

    def joined(parts):
        top = jnp.max(parts, axis=0)
        return top + jnp.log(jnp.sum(jnp.exp(parts - top[None]), axis=0))

    join_rows(lcol, 0, c1x, c2x, c3x, joined, p_recv)
    run_s[...] = jnp.zeros_like(run_s)

    def rows(step, carry):
        part = part_at(GROUP - 1 - step)

        @pl.when(step > 0)
        def _():
            drain(c3x.at[part], p_recv.at[part])

        at = pl.ds(pl.multiple_of(part * 8, 8), 8)
        level = lc_ref[at, :] - c3x[part]
        gcol[at, :] = level
        scale = jnp.exp(level + mloc[at, :])
        u[at, :] = scale
        total = run_s[...]
        for k in range(8):
            total = total + w[:, tile(part * 8 + k)] * scale[k : k + 1, :]
        run_s[...] = total
        return carry

    lax.fori_loop(0, GROUP, rows, 0)
    line = jnp.sum(run_s[...].T, axis=0, keepdims=True)
    lines = swap_cols(line, 1, rx2)
    total = jnp.sum(lines, axis=0)
    f2 = lr_ref[...] + f1 - jnp.log(total)
    row_out[...] = rc_ref[...] + EPSILON * f2
    bcast[...] = spread(jnp.exp(lr_ref[...]) / total)

    def second_columns(b, at):
        sums = [jnp.sum(w[:, tile(b + k)] * bcast[...], axis=0, keepdims=True) for k in range(8)]
        lcol2[at, :] = jnp.concatenate(sums, axis=0) * u[at, :]

    column_parts(second_columns, lcol2, 1, d1x)
    join_rows(lcol2, 1, d1x, d2x, d3x, lambda parts: jnp.sum(parts, axis=0), q_recv)

    def result(step, carry):
        part = part_at(GROUP - 1 - step)

        @pl.when(step > 0)
        def _():
            drain(d3x.at[part], q_recv.at[part])

        at = pl.ds(pl.multiple_of(part * 8, 8), 8)
        level = lc_ref[at, :] + gcol[at, :] - jnp.log(d3x[part])
        col_out[at, :] = cc_ref[at, :] + EPSILON * level
        return carry

    lax.fori_loop(0, GROUP, result, 0)

    drain(tg.at[pl.ds(0, COLS - 1)], t_sems.at[0])
    drain(c1g.at[pl.ds(0, COLS - 1)], c1_sems.at[0])
    drain(tfull.at[pl.ds(0, CHIPS - 1), 0], tf_sems.at[0])
    drain(tfull.at[:, 0], tf_sems.at[2])
    for half in range(2):
        drain(c2c.at[:, pl.ds(0, ROWS - 1)], a_send.at[half])
    drain(ybuf.at[pl.ds(0, 12)], yp_send)
    drain(ybuf.at[pl.ds(0, 12)], ym_send)
    drain(ybuf.at[pl.ds(0, 6)], zz_send)
    drain(ybuf.at[pl.ds(0, 32)], core_send)
    for slot in range(2):
        drain(rx1.at[pl.ds(0, COLS - 1)], r_send.at[slot])
        drain(c1x.at[pl.ds(0, GROUP - 1)], x_send.at[slot, 0])
        drain(c2x.at[pl.ds(0, NZ - 1)], x_send.at[slot, 1])
        drain(c3x.at[pl.ds(0, GROUP - 1)], x_send.at[slot, 2])


def handed_on(*refs):
    for source, target in zip(refs[:3], refs[3:]):
        target[...] = source[...]


def body(y_prev, t_block, c2_panel, c1_panel, z_prev, row_const, col_const, log_row_mass, log_col_mass, col_warm):
    tall = lambda a: a.reshape(TILES, LANES)
    flat = lambda a: a.reshape(1, HEIGHT)
    hbm = pl.BlockSpec(memory_space=pl.ANY)
    vmem = pl.BlockSpec(memory_space=pltpu.VMEM)
    dma = pltpu.SemaphoreType.DMA
    y_next, row_pot, col_pot = pl.pallas_call(
        kernel,
        out_shape=(
            jax.ShapeDtypeStruct((DEPTH, WIDTH), F32),
            jax.ShapeDtypeStruct((1, HEIGHT), F32),
            jax.ShapeDtypeStruct((TILES, LANES), F32),
        ),
        in_specs=[hbm, vmem, hbm, hbm, hbm] + [vmem] * 5,
        out_specs=(vmem, vmem, vmem),
        scratch_shapes=[
            pltpu.VMEM((HEIGHT, WIDTH), F32),
            pltpu.VMEM((TILES, PANEL, LANES), F32),
            pltpu.VMEM((2, ROWS, DEPTH, LANES), F32),
            pltpu.VMEM((2, ROWS, DEPTH, LANES), F32),
            pltpu.VMEM((DEPTH, LANES), F32),
            pltpu.VMEM((COLS, DEPTH, LANES), F32),
            pltpu.VMEM((DEPTH, PANEL), F32),
            pltpu.VMEM((CHIPS, 2, DEPTH, PANEL), F32),
            pltpu.VMEM((COLS, T_COLS, HEIGHT), F32),
            pltpu.VMEM((HEIGHT, 3 * PANEL), BF16),
            pltpu.VMEM((TILES, LANES), F32),
            pltpu.VMEM((HEIGHT, LANES), F32),
            pltpu.VMEM((HEIGHT, LANES), F32),
            pltpu.VMEM((HEIGHT, LANES), F32),
            pltpu.VMEM((2, 1, HEIGHT), F32),
            pltpu.VMEM((COLS, 1, HEIGHT), F32),
            pltpu.VMEM((COLS, 1, HEIGHT), F32),
            pltpu.VMEM((TILES, LANES), F32),
            pltpu.VMEM((TILES, LANES), F32),
            pltpu.VMEM((TILES, LANES), F32),
            pltpu.VMEM((2, 8, LANES), F32),
            pltpu.VMEM((2, 8, LANES), F32),
            pltpu.VMEM((TILES, LANES), F32),
            pltpu.VMEM((GROUP, 8, LANES), F32),
            pltpu.VMEM((NZ, 8, LANES), F32),
            pltpu.VMEM((GROUP, 8, LANES), F32),
            pltpu.VMEM((GROUP, 8, LANES), F32),
            pltpu.VMEM((NZ, 8, LANES), F32),
            pltpu.VMEM((GROUP, 8, LANES), F32),
            dma,
            dma((2,)),
            dma((2,)),
            dma((4,)),
            dma((2,)),
            dma((2,)),
            dma((TILES,)),
            dma,
            dma,
            dma,
            dma,
            dma((2,)),
            dma((2,)),
            dma((2, 3)),
            dma((2, 2)),
            dma((GROUP,)),
            dma((GROUP,)),
        ],
        compiler_params=pltpu.CompilerParams(
            collective_id=0, has_side_effects=True, vmem_limit_bytes=56 * 1024 * 1024
        ),
        name="step",
    )(
        y_prev, t_block, c2_panel, c1_panel.T, z_prev, flat(row_const), tall(col_const),
        flat(log_row_mass), tall(log_col_mass), tall(col_warm),
    )
    y_next, row_pot, col_pot = pl.pallas_call(
        handed_on,
        out_shape=(
            jax.ShapeDtypeStruct((DEPTH, WIDTH), F32),
            jax.ShapeDtypeStruct((1, HEIGHT), F32),
            jax.ShapeDtypeStruct((TILES, LANES), F32),
        ),
        in_specs=[vmem] * 3,
        out_specs=(vmem, vmem, vmem),
        name="results",
    )(y_next, row_pot, col_pot)
    return y_next, row_pot.reshape(HEIGHT), col_pot.reshape(WIDTH)


def solution(mesh):
    block = P("row", "col")
    return jax.shard_map(
        body,
        mesh=mesh,
        in_specs=(block,) * 5 + (P("row"), P("col"), P("row"), P("col"), P("col")),
        out_specs=(block, P("row"), P("col")),
        check_vma=False,
    )
```

```python
import jax
import jax.numpy as jnp
from jax import lax
from jax.experimental import pallas as pl
from jax.experimental.pallas import tpu as pltpu
from jax.sharding import PartitionSpec as P

MESH = pl.DeviceIdType.MESH
F32 = jnp.float32
BF16 = jnp.bfloat16
ROWS, COLS = 32, 8
NZ, NY = 4, 4
GROUP = 8
CHIPS = NZ * NY
PANEL = 256
HEIGHT = 256
WIDTH = 8192
LANES = 128
TILES = WIDTH // LANES
DEPTH = PANEL // ROWS
T_COLS = PANEL // COLS
EPSILON = 5.0
LOW = -1e30
STRIP = 64
LOG2E = 1.4426950408889634
BEHIND = 1

ORDER = (
    (0, 0, 0), (3, 0, 0), (1, 0, 0), (0, 0, 1),
    (0, 3, 0), (0, 1, 0), (2, 0, 0), (3, 0, 1), (1, 0, 1),
    (0, 3, 1), (0, 1, 1), (3, 3, 0), (1, 3, 0), (3, 1, 0), (1, 1, 0),
    (2, 0, 1), (0, 2, 0), (0, 2, 1),
    (3, 3, 1), (1, 3, 1), (3, 1, 1), (1, 1, 1),
    (2, 3, 0), (2, 1, 0), (3, 2, 0), (1, 2, 0), (3, 2, 1), (1, 2, 1),
    (2, 3, 1), (2, 1, 1), (2, 2, 0), (2, 2, 1),
)


def entry(index):
    found = jnp.int32(0)
    for k, (dy, dz, half) in enumerate(ORDER):
        if k:
            found = jnp.where(index == k, jnp.int32(dy * 8 + dz * 2 + half), found)
    return found


def log2(a):
    return jnp.log(a) * LOG2E


def three_left(a):
    high = a.astype(BF16)
    low = (a - high.astype(F32)).astype(BF16)
    return jnp.concatenate([high, low, high], axis=1)


def three_right(b):
    high = b.astype(BF16)
    low = (b - high.astype(F32)).astype(BF16)
    return jnp.concatenate([high, high, low], axis=0)


def kernel(
    yp_hbm, t_hbm, c2_hbm, c1_hbm, zp_hbm, rc_hbm, cc_hbm, lr_hbm, lc_hbm, cw_hbm,
    y_hbm, row_out, col_out,
    t_ref, rc_ref, cc_ref, lr_ref, lc_ref, cw_ref, y_out, in_sems, y_sem,
    w, ybuf, c2c, ypc, tline, tslab, tall, twhole, c1g, left, gcol, run_m, run_s, bcast,
    sx, rx1, rx2, mloc, lcol, lcol2, part1, part2, u, c1x, c2x, c3x, d1x, d2x, d3x,
    z_sem, t_sems, c1_sems, tf_sems, a_send, a_recv, y_recv, yp_send, ym_send, zz_send, core_send,
    r_send, r_recv, x_send, x_recv, p_recv, q_recv,
):
    r, q = lax.axis_index("row"), lax.axis_index("col")
    zh, yy, core = r // GROUP, (r // 2) % NY, r % 2
    g = r % GROUP

    def row_at(dz, dy, c):
        return ((zh + dz) % NZ * NY + (yy + dy) % NY) * 2 + c

    def remote(src, dst, send, recv, row, col):
        return pltpu.make_async_remote_copy(
            src_ref=src, dst_ref=dst, send_sem=send, recv_sem=recv,
            device_id=(row, col), device_id_type=MESH,
        )

    def drain(ref, sem):
        pltpu.make_async_copy(ref, ref, sem).wait()

    def other_rows(do):
        def one(j, carry):
            do((r + j) % ROWS)
            return carry

        lax.fori_loop(1, ROWS, one, 0)

    def other_cols(do):
        def one(j, carry):
            do((q + j) % COLS)
            return carry

        lax.fori_loop(1, COLS, one, 0)

    small = ((rc_hbm, rc_ref), (cc_hbm, cc_ref), (lr_hbm, lr_ref), (lc_hbm, lc_ref), (cw_hbm, cw_ref))
    pltpu.make_async_copy(t_hbm, t_ref, in_sems.at[0]).start()
    for k, (source, target) in enumerate(small):
        pltpu.make_async_copy(source, target, in_sems.at[k + 1]).start()

    barrier = pltpu.get_barrier_semaphore()

    def greet(row, col):
        pl.semaphore_signal(barrier, inc=1, device_id=(row, col), device_id_type=MESH)

    other_cols(lambda col: greet(r, col))
    other_rows(lambda row: greet(row, q))
    pltpu.make_async_copy(zp_hbm, w, z_sem).start()
    drain(t_ref, in_sems.at[0])
    tline[...] = jnp.concatenate([t_ref[k : k + 1, :] for k in range(DEPTH)], axis=1)
    pl.semaphore_wait(barrier, ROWS + COLS - 2)

    other_rows(lambda row: remote(tline, tslab.at[r], t_sems.at[0], t_sems.at[1], row, q).start())
    pltpu.make_async_copy(tline, tslab.at[r], t_sems.at[1]).start()

    def scatter(half, which):
        def columns(row):
            return pl.ds(pl.multiple_of(row * 2 * LANES + half * LANES, LANES), LANES)

        k = half * 2 + which
        src, dst = ((c2_hbm, c2c), (yp_hbm, ypc))[which]

        def send(row):
            remote(src.at[:, columns(row)], dst.at[half, r], a_send.at[k], a_recv.at[k], row, q).start()

        other_rows(send)
        pltpu.make_async_copy(src.at[:, columns(r)], dst.at[half, r], a_recv.at[k]).start()

    scatter(0, 0)
    scatter(0, 1)

    scatter(1, 0)
    scatter(1, 1)
    mine = pl.ds(pl.multiple_of(r * DEPTH, DEPTH), DEPTH)

    drain(tslab, t_sems.at[1])
    other_cols(lambda col: remote(tslab, tall.at[q], tf_sems.at[0], tf_sems.at[1], r, col).start())
    pltpu.make_async_copy(tslab, tall.at[q], tf_sems.at[1]).start()
    pltpu.make_async_copy(c1_hbm, c1g.at[q], c1_sems.at[1]).start()
    other_cols(lambda col: remote(c1_hbm, c1g.at[q], c1_sems.at[0], c1_sems.at[1], r, col).start())

    for k, (_, target) in enumerate(small):
        drain(target, in_sems.at[k + 1])
    gcol[...] = cw_ref[...] * (LOG2E / EPSILON)
    run_m[...] = jnp.full_like(run_m, LOW)
    run_s[...] = jnp.zeros_like(run_s)

    drain(tall, tf_sems.at[1])
    slabs = [tall[k].reshape(ROWS, DEPTH * T_COLS) for k in range(COLS)]
    for k in range(DEPTH):
        rows_k = jnp.concatenate([slab[:, k * T_COLS : (k + 1) * T_COLS] for slab in slabs], axis=1)
        for side in range(PANEL // LANES):
            twhole[side, pl.ds(k, ROWS, DEPTH), :] = rows_k[:, side * LANES : (side + 1) * LANES]
    t_three = three_left(jnp.concatenate([twhole[side] for side in range(PANEL // LANES)], axis=1))
    left[...] = t_three

    def own_block(half):
        drain(c2c.at[half], a_recv.at[half * 2])
        block = jnp.dot(
            left[...], three_right(c2c[half].reshape(PANEL, LANES)), preferred_element_type=F32
        )
        drain(ypc.at[half], a_recv.at[half * 2 + 1])
        ybuf[r * 2 + half] = ypc[half].reshape(PANEL, LANES) + block

    def block_at(dz, dy, c, half):
        return row_at(dz, dy, c) * 2 + half

    def pass_on(dz, dy, half):
        b = block_at(dz, dy, core, half)
        here = ybuf.at[b]
        near, first = dy == 0, half == 0
        start = near & (dz == 0)

        def hand(condition, send, row):
            @pl.when(condition)
            def _():
                remote(here, here, send, y_recv.at[b], row, q).start()

        @pl.when(~start)
        def _():
            pltpu.make_async_copy(here, here, y_recv.at[b]).wait()

        hand(near | ((dy == NY - 1) & first), yp_send, row_at(0, 1, core))
        hand(near | ((dy == 1) & ~first), ym_send, row_at(0, NY - 1, core))
        hand(start | (near & (dz == NZ - 1) & first), zz_send, row_at(1, 0, core))
        hand(start | (near & (dz == 1) & ~first), zz_send, row_at(NZ - 1, 0, core))
        remote(here, here, core_send, y_recv.at[b], row_at(0, 0, 1 - core), q).start()

    def parted(code):
        return code // 8, code // 2 % 4, code % 2

    def take(code):
        dy, dz, half = parted(code)
        first, second = block_at(dz, dy, core, half), block_at(dz, dy, 1 - core, half)
        pltpu.make_async_copy(ybuf.at[second], ybuf.at[second], y_recv.at[second]).wait()
        for b in (first, second):
            y_out[:, pl.ds(pl.multiple_of(b * LANES, LANES), LANES)] = ybuf[b, mine, :]
        both = jnp.concatenate([ybuf[first], ybuf[second]], axis=1)
        product = jnp.dot(left[...], three_right(both), preferred_element_type=F32)
        scores = []
        for side, b in enumerate((first, second)):
            at = pl.ds(pl.multiple_of(b * LANES, LANES), LANES)
            level = (2.0 / EPSILON * LOG2E) * (w[:, at] + product[:, side * LANES : (side + 1) * LANES])
            w[:, at] = level
            scores.append(level + gcol[pl.ds(b, 1), :])
        before = run_m[...]
        peak = jnp.maximum(before, jnp.maximum(scores[0], scores[1]))
        total = run_s[...] * jnp.exp2(before - peak)
        run_s[...] = total + jnp.exp2(scores[0] - peak) + jnp.exp2(scores[1] - peak)
        run_m[...] = peak

    own_block(0)

    def event(index, before):
        code = entry(index)
        dy, dz, half = parted(code)

        @pl.when(index < len(ORDER))
        def _():
            pass_on(dz, dy, half)

        @pl.when(index == 0)
        def _():
            own_block(1)
            drain(c1g, c1_sems.at[1])
            drain(w, z_sem)
            left[...] = three_left(c1g[...].reshape(PANEL, HEIGHT).T)

        @pl.when(index >= BEHIND)
        def _():
            take(before[-1])

        return (code, *before[:-1])

    lax.fori_loop(0, len(ORDER) + BEHIND, event, (jnp.int32(0),) * BEHIND)

    pltpu.make_async_copy(y_out, y_hbm, y_sem).start()

    def spread(line):
        return jnp.broadcast_to(line, (LANES, HEIGHT)).T

    def swap_cols(value, slot, buffer):
        sx[slot] = value
        buffer[q] = value
        other_cols(
            lambda col: remote(
                sx.at[slot], buffer.at[q], r_send.at[slot], r_recv.at[slot], r, col
            ).start()
        )
        rest = buffer.at[pl.ds(0, COLS - 1)]
        drain(rest, r_recv.at[slot])
        return buffer[...]

    m_t, s_t = run_m[...].T, run_s[...].T
    peak = jnp.max(m_t, axis=0, keepdims=True)
    line = peak + log2(jnp.sum(s_t * jnp.exp2(m_t - peak), axis=0, keepdims=True))
    lines = swap_cols(line, 0, rx1)
    peak = jnp.max(lines, axis=0)
    f1 = LOG2E * lr_ref[...] - peak - log2(jnp.sum(jnp.exp2(lines - peak[None]), axis=0))
    bcast[...] = spread(f1)

    def tile(b):
        return pl.ds(pl.multiple_of(b * LANES, LANES), LANES)

    def part_at(j):
        pair = j // 2
        dy = jnp.where(pair == 0, 2, jnp.where(pair == 1, 1, jnp.where(pair == 2, 3, 0)))
        return (yy + dy) % NY * 2 + (core + 1 + j) % 2

    def column_parts(work, source, slot, first):
        def one(j, carry):
            part = part_at(j)
            at = pl.ds(pl.multiple_of(part * 8, 8), 8)
            work(part * 8, at)

            @pl.when(j < GROUP - 1)
            def _():
                remote(
                    source.at[at, :], first.at[g], x_send.at[slot, 0], x_recv.at[slot, 0],
                    zh * GROUP + part, q,
                ).start()

            return carry

        lax.fori_loop(0, GROUP, one, 0)

    def over_strips(value, join):
        joined = [
            join(value(pl.ds(at, STRIP)).reshape(STRIP // 8, 8, LANES), axis=0)
            for at in range(0, HEIGHT, STRIP)
        ]
        return join(jnp.stack(joined), axis=0)

    def first_columns(b, at):
        tops, sums = [], []
        for k in range(8):
            cut = tile(b + k)
            tops.append(
                jnp.max(over_strips(lambda rows: w[rows, cut] + bcast[rows, :], jnp.max), axis=0, keepdims=True)
            )
        for k in range(8):
            cut = tile(b + k)

            def scaled(rows):
                value = jnp.exp2(w[rows, cut] + (bcast[rows, :] - tops[k]))
                w[rows, cut] = value
                return value

            sums.append(jnp.sum(over_strips(scaled, jnp.sum), axis=0, keepdims=True))
        top = jnp.concatenate(tops, axis=0)
        mloc[at, :] = top
        lcol[at, :] = top + log2(jnp.concatenate(sums, axis=0))

    column_parts(first_columns, lcol, 0, c1x)

    def join_rows(source, slot, first, second, third, join, p_recv):
        first[g] = source[pl.ds(pl.multiple_of(g * 8, 8), 8), :]
        drain(first.at[pl.ds(0, GROUP - 1)], x_recv.at[slot, 0])
        part = join(first[...])
        part1[slot] = part
        for dz in (2, 1, 3):
            remote(
                part1.at[slot], second.at[zh], x_send.at[slot, 1], x_recv.at[slot, 1],
                row_at(dz, 0, core), q,
            ).start()
        second[zh] = part
        drain(second.at[pl.ds(0, NZ - 1)], x_recv.at[slot, 1])
        whole = join(second[...])
        part2[slot] = whole

        def one(j, carry):
            row = zh * GROUP + part_at(j)
            remote(part2.at[slot], third.at[g], x_send.at[slot, 2], p_recv.at[g], row, q).start()
            return carry

        lax.fori_loop(0, GROUP - 1, one, 0)
        third[g] = whole

    def joined(parts):
        top = jnp.max(parts, axis=0)
        return top + log2(jnp.sum(jnp.exp2(parts - top[None]), axis=0))

    join_rows(lcol, 0, c1x, c2x, c3x, joined, p_recv)
    run_s[...] = jnp.zeros_like(run_s)

    def rows(step, carry):
        part = part_at(GROUP - 1 - step)

        @pl.when(step > 0)
        def _():
            drain(c3x.at[part], p_recv.at[part])

        at = pl.ds(pl.multiple_of(part * 8, 8), 8)
        level = LOG2E * lc_ref[at, :] - c3x[part]
        gcol[at, :] = level
        scale = jnp.exp2(level + mloc[at, :])
        u[at, :] = scale
        for top in range(0, HEIGHT, STRIP):
            strip = pl.ds(top, STRIP)
            total = run_s[strip, :]
            for k in range(8):
                total = total + w[strip, tile(part * 8 + k)] * scale[k : k + 1, :]
            run_s[strip, :] = total
        return carry

    lax.fori_loop(0, GROUP, rows, 0)
    line = jnp.sum(run_s[...].T, axis=0, keepdims=True)
    lines = swap_cols(line, 1, rx2)
    total = jnp.sum(lines, axis=0)
    f2 = LOG2E * lr_ref[...] + f1 - log2(total)
    row_out[...] = rc_ref[...] + EPSILON / LOG2E * f2
    bcast[...] = spread(jnp.exp(lr_ref[...]) / total)

    def second_columns(b, at):
        sums = [jnp.zeros((8, LANES), F32)] * 8
        for top in range(0, HEIGHT, STRIP):
            strip = pl.ds(top, STRIP)
            weight = bcast[strip, :]
            for k in range(8):
                product = w[strip, tile(b + k)] * weight
                sums[k] = sums[k] + jnp.sum(product.reshape(STRIP // 8, 8, LANES), axis=0)
        sums = [jnp.sum(value, axis=0, keepdims=True) for value in sums]
        lcol2[at, :] = jnp.concatenate(sums, axis=0) * u[at, :]

    column_parts(second_columns, lcol2, 1, d1x)
    join_rows(lcol2, 1, d1x, d2x, d3x, lambda parts: jnp.sum(parts, axis=0), q_recv)

    def result(step, carry):
        part = part_at(GROUP - 1 - step)

        @pl.when(step > 0)
        def _():
            drain(d3x.at[part], q_recv.at[part])

        at = pl.ds(pl.multiple_of(part * 8, 8), 8)
        level = LOG2E * lc_ref[at, :] + gcol[at, :] - log2(d3x[part])
        col_out[at, :] = cc_ref[at, :] + EPSILON / LOG2E * level
        return carry

    lax.fori_loop(0, GROUP, result, 0)

    drain(y_out, y_sem)
    drain(tslab.at[pl.ds(0, ROWS - 1)], t_sems.at[0])
    drain(c1g.at[pl.ds(0, COLS - 1)], c1_sems.at[0])
    drain(tall.at[pl.ds(0, COLS - 1)], tf_sems.at[0])
    for k in range(4):
        drain(c2c.at[0, pl.ds(0, ROWS - 1)], a_send.at[k])
    drain(ybuf.at[pl.ds(0, 12)], yp_send)
    drain(ybuf.at[pl.ds(0, 12)], ym_send)
    drain(ybuf.at[pl.ds(0, 6)], zz_send)
    drain(ybuf.at[pl.ds(0, 32)], core_send)
    for slot in range(2):
        drain(rx1.at[pl.ds(0, COLS - 1)], r_send.at[slot])
        drain(c1x.at[pl.ds(0, GROUP - 1)], x_send.at[slot, 0])
        drain(c2x.at[pl.ds(0, NZ - 1)], x_send.at[slot, 1])
        drain(c3x.at[pl.ds(0, GROUP - 1)], x_send.at[slot, 2])


def handed_on(*refs):
    for source, target in zip(refs[:3], refs[3:]):
        target[...] = source[...]


def body(y_prev, t_block, c2_panel, c1_panel, z_prev, row_const, col_const, log_row_mass, log_col_mass, col_warm):
    tall = lambda a: a.reshape(TILES, LANES)
    flat = lambda a: a.reshape(1, HEIGHT)
    hbm = pl.BlockSpec(memory_space=pl.ANY)
    vmem = pl.BlockSpec(memory_space=pltpu.VMEM)
    dma = pltpu.SemaphoreType.DMA
    y_next, row_pot, col_pot = pl.pallas_call(
        kernel,
        out_shape=(
            jax.ShapeDtypeStruct((DEPTH, WIDTH), F32),
            jax.ShapeDtypeStruct((1, HEIGHT), F32),
            jax.ShapeDtypeStruct((TILES, LANES), F32),
        ),
        in_specs=[hbm] * 10,
        out_specs=(hbm, vmem, vmem),
        scratch_shapes=[
            pltpu.VMEM((DEPTH, T_COLS), F32),
            pltpu.VMEM((1, HEIGHT), F32),
            pltpu.VMEM((TILES, LANES), F32),
            pltpu.VMEM((1, HEIGHT), F32),
            pltpu.VMEM((TILES, LANES), F32),
            pltpu.VMEM((TILES, LANES), F32),
            pltpu.VMEM((DEPTH, WIDTH), F32),
            dma((6,)),
            dma,
            pltpu.VMEM((HEIGHT, WIDTH), F32),
            pltpu.VMEM((TILES, PANEL, LANES), F32),
            pltpu.VMEM((2, ROWS, DEPTH, LANES), F32),
            pltpu.VMEM((2, ROWS, DEPTH, LANES), F32),
            pltpu.VMEM((1, PANEL), F32),
            pltpu.VMEM((ROWS, 1, PANEL), F32),
            pltpu.VMEM((COLS, ROWS, 1, PANEL), F32),
            pltpu.VMEM((PANEL // LANES, PANEL, LANES), F32),
            pltpu.VMEM((COLS, T_COLS, HEIGHT), F32),
            pltpu.VMEM((HEIGHT, 3 * PANEL), BF16),
            pltpu.VMEM((TILES, LANES), F32),
            pltpu.VMEM((HEIGHT, LANES), F32),
            pltpu.VMEM((HEIGHT, LANES), F32),
            pltpu.VMEM((HEIGHT, LANES), F32),
            pltpu.VMEM((2, 1, HEIGHT), F32),
            pltpu.VMEM((COLS, 1, HEIGHT), F32),
            pltpu.VMEM((COLS, 1, HEIGHT), F32),
            pltpu.VMEM((TILES, LANES), F32),
            pltpu.VMEM((TILES, LANES), F32),
            pltpu.VMEM((TILES, LANES), F32),
            pltpu.VMEM((2, 8, LANES), F32),
            pltpu.VMEM((2, 8, LANES), F32),
            pltpu.VMEM((TILES, LANES), F32),
            pltpu.VMEM((GROUP, 8, LANES), F32),
            pltpu.VMEM((NZ, 8, LANES), F32),
            pltpu.VMEM((GROUP, 8, LANES), F32),
            pltpu.VMEM((GROUP, 8, LANES), F32),
            pltpu.VMEM((NZ, 8, LANES), F32),
            pltpu.VMEM((GROUP, 8, LANES), F32),
            dma,
            dma((2,)),
            dma((2,)),
            dma((2,)),
            dma((4,)),
            dma((4,)),
            dma((TILES,)),
            dma,
            dma,
            dma,
            dma,
            dma((2,)),
            dma((2,)),
            dma((2, 3)),
            dma((2, 2)),
            dma((GROUP,)),
            dma((GROUP,)),
        ],
        compiler_params=pltpu.CompilerParams(
            collective_id=0, has_side_effects=True, vmem_limit_bytes=56 * 1024 * 1024
        ),
        name="step",
    )(
        y_prev, t_block, c2_panel, c1_panel.T, z_prev, flat(row_const), tall(col_const),
        flat(log_row_mass), tall(log_col_mass), tall(col_warm),
    )
    y_next, row_pot, col_pot = pl.pallas_call(
        handed_on,
        out_shape=(
            jax.ShapeDtypeStruct((DEPTH, WIDTH), F32),
            jax.ShapeDtypeStruct((1, HEIGHT), F32),
            jax.ShapeDtypeStruct((TILES, LANES), F32),
        ),
        in_specs=[vmem] * 3,
        out_specs=(vmem, vmem, vmem),
        name="results",
    )(y_next, row_pot, col_pot)
    return y_next, row_pot.reshape(HEIGHT), col_pot.reshape(WIDTH)


def solution(mesh):
    block = P("row", "col")
    return jax.shard_map(
        body,
        mesh=mesh,
        in_specs=(block,) * 5 + (P("row"), P("col"), P("row"), P("col"), P("col")),
        out_specs=(block, P("row"), P("col")),
        check_vma=False,
    )
```

```python
import jax
import jax.numpy as jnp
from jax import lax
from jax.experimental import pallas as pl
from jax.experimental.pallas import tpu as pltpu
from jax.sharding import PartitionSpec as P

MESH = pl.DeviceIdType.MESH
F32 = jnp.float32
BF16 = jnp.bfloat16
ROWS, COLS = 32, 8
NZ, NY = 4, 4
GROUP = 8
CHIPS = NZ * NY
PANEL = 256
HEIGHT = 256
WIDTH = 8192
LANES = 128
TILES = WIDTH // LANES
DEPTH = PANEL // ROWS
T_COLS = PANEL // COLS
EPSILON = 5.0
LOW = -1e30
STRIP = 128
LOG2E = 1.4426950408889634
BEHIND = 1

ORDER = (
    (0, 0, 0), (3, 0, 0), (1, 0, 0), (0, 0, 1),
    (0, 3, 0), (0, 1, 0), (2, 0, 0), (3, 0, 1), (1, 0, 1),
    (0, 3, 1), (0, 1, 1), (3, 3, 0), (1, 3, 0), (3, 1, 0), (1, 1, 0),
    (2, 0, 1), (0, 2, 0), (0, 2, 1),
    (3, 3, 1), (1, 3, 1), (3, 1, 1), (1, 1, 1),
    (2, 3, 0), (2, 1, 0), (3, 2, 0), (1, 2, 0), (3, 2, 1), (1, 2, 1),
    (2, 3, 1), (2, 1, 1), (2, 2, 0), (2, 2, 1),
)


def entry(index):
    found = jnp.int32(0)
    for k, (dy, dz, half) in enumerate(ORDER):
        if k:
            found = jnp.where(index == k, jnp.int32(dy * 8 + dz * 2 + half), found)
    return found


def log2(a):
    return jnp.log(a) * LOG2E


def three_left(a):
    high = a.astype(BF16)
    low = (a - high.astype(F32)).astype(BF16)
    return jnp.concatenate([high, low, high], axis=1)


def three_right(b):
    high = b.astype(BF16)
    low = (b - high.astype(F32)).astype(BF16)
    return jnp.concatenate([high, high, low], axis=0)


def kernel(
    yp_hbm, t_hbm, c2_hbm, c1_hbm, zp_hbm, rc_hbm, cc_hbm, lr_hbm, lc_hbm, cw_hbm,
    y_hbm, row_out, col_out,
    t_ref, rc_ref, cc_ref, lr_ref, lc_ref, cw_ref, y_out, in_sems, y_sem,
    w, ybuf, c2c, ypc, tline, tslab, tall, twhole, c1g, left, gcol, run_m, run_s, bcast,
    sx, rx1, rx2, mloc, lcol, lcol2, part1, part2, u, c1x, c2x, c3x, d1x, d2x, d3x,
    z_sem, t_sems, c1_sems, tf_sems, a_send, a_recv, y_recv, yp_send, ym_send, zz_send, core_send,
    r_send, r_recv, x_send, x_recv, p_recv, q_recv,
):
    r, q = lax.axis_index("row"), lax.axis_index("col")
    zh, yy, core = r // GROUP, (r // 2) % NY, r % 2
    g = r % GROUP

    def row_at(dz, dy, c):
        return ((zh + dz) % NZ * NY + (yy + dy) % NY) * 2 + c

    def remote(src, dst, send, recv, row, col):
        return pltpu.make_async_remote_copy(
            src_ref=src, dst_ref=dst, send_sem=send, recv_sem=recv,
            device_id=(row, col), device_id_type=MESH,
        )

    def drain(ref, sem):
        pltpu.make_async_copy(ref, ref, sem).wait()

    def other_rows(do):
        def one(j, carry):
            do((r + j) % ROWS)
            return carry

        lax.fori_loop(1, ROWS, one, 0)

    def other_cols(do):
        def one(j, carry):
            do((q + j) % COLS)
            return carry

        lax.fori_loop(1, COLS, one, 0)

    small = ((rc_hbm, rc_ref), (cc_hbm, cc_ref), (lr_hbm, lr_ref), (lc_hbm, lc_ref), (cw_hbm, cw_ref))
    pltpu.make_async_copy(t_hbm, t_ref, in_sems.at[0]).start()
    for k, (source, target) in enumerate(small):
        pltpu.make_async_copy(source, target, in_sems.at[k + 1]).start()

    barrier = pltpu.get_barrier_semaphore()

    def greet(row, col):
        pl.semaphore_signal(barrier, inc=1, device_id=(row, col), device_id_type=MESH)

    other_cols(lambda col: greet(r, col))
    other_rows(lambda row: greet(row, q))
    pltpu.make_async_copy(zp_hbm, w, z_sem).start()
    drain(t_ref, in_sems.at[0])
    tline[...] = jnp.concatenate([t_ref[k : k + 1, :] for k in range(DEPTH)], axis=1)
    pl.semaphore_wait(barrier, ROWS + COLS - 2)

    other_rows(lambda row: remote(tline, tslab.at[r], t_sems.at[0], t_sems.at[1], row, q).start())
    pltpu.make_async_copy(tline, tslab.at[r], t_sems.at[1]).start()

    def scatter(half, which):
        def columns(row):
            return pl.ds(pl.multiple_of(row * 2 * LANES + half * LANES, LANES), LANES)

        k = half * 2 + which
        src, dst = ((c2_hbm, c2c), (yp_hbm, ypc))[which]

        def send(row):
            remote(src.at[:, columns(row)], dst.at[half, r], a_send.at[k], a_recv.at[k], row, q).start()

        other_rows(send)
        pltpu.make_async_copy(src.at[:, columns(r)], dst.at[half, r], a_recv.at[k]).start()

    scatter(0, 0)
    scatter(0, 1)

    scatter(1, 0)
    scatter(1, 1)
    mine = pl.ds(pl.multiple_of(r * DEPTH, DEPTH), DEPTH)

    drain(tslab, t_sems.at[1])
    other_cols(lambda col: remote(tslab, tall.at[q], tf_sems.at[0], tf_sems.at[1], r, col).start())
    pltpu.make_async_copy(tslab, tall.at[q], tf_sems.at[1]).start()
    pltpu.make_async_copy(c1_hbm, c1g.at[q], c1_sems.at[1]).start()
    other_cols(lambda col: remote(c1_hbm, c1g.at[q], c1_sems.at[0], c1_sems.at[1], r, col).start())

    for k, (_, target) in enumerate(small):
        drain(target, in_sems.at[k + 1])
    gcol[...] = cw_ref[...] * (LOG2E / EPSILON)
    run_m[...] = jnp.full_like(run_m, LOW)
    run_s[...] = jnp.zeros_like(run_s)

    drain(tall, tf_sems.at[1])
    slabs = [tall[k].reshape(ROWS, DEPTH * T_COLS) for k in range(COLS)]
    for k in range(DEPTH):
        rows_k = jnp.concatenate([slab[:, k * T_COLS : (k + 1) * T_COLS] for slab in slabs], axis=1)
        for side in range(PANEL // LANES):
            twhole[side, pl.ds(k, ROWS, DEPTH), :] = rows_k[:, side * LANES : (side + 1) * LANES]
    t_three = three_left(jnp.concatenate([twhole[side] for side in range(PANEL // LANES)], axis=1))
    left[...] = t_three

    def own_block(half):
        drain(c2c.at[half], a_recv.at[half * 2])
        block = jnp.dot(
            left[...], three_right(c2c[half].reshape(PANEL, LANES)), preferred_element_type=F32
        )
        drain(ypc.at[half], a_recv.at[half * 2 + 1])
        ybuf[r * 2 + half] = ypc[half].reshape(PANEL, LANES) + block

    def block_at(dz, dy, c, half):
        return row_at(dz, dy, c) * 2 + half

    def pass_on(dz, dy, half):
        b = block_at(dz, dy, core, half)
        here = ybuf.at[b]
        near, first = dy == 0, half == 0
        start = near & (dz == 0)

        def hand(condition, send, row):
            @pl.when(condition)
            def _():
                remote(here, here, send, y_recv.at[b], row, q).start()

        @pl.when(~start)
        def _():
            pltpu.make_async_copy(here, here, y_recv.at[b]).wait()

        hand(near | ((dy == NY - 1) & first), yp_send, row_at(0, 1, core))
        hand(near | ((dy == 1) & ~first), ym_send, row_at(0, NY - 1, core))
        hand(start | (near & (dz == NZ - 1) & first), zz_send, row_at(1, 0, core))
        hand(start | (near & (dz == 1) & ~first), zz_send, row_at(NZ - 1, 0, core))
        remote(here, here, core_send, y_recv.at[b], row_at(0, 0, 1 - core), q).start()

    def parted(code):
        return code // 8, code // 2 % 4, code % 2

    def take(code):
        dy, dz, half = parted(code)
        first, second = block_at(dz, dy, core, half), block_at(dz, dy, 1 - core, half)
        pltpu.make_async_copy(ybuf.at[second], ybuf.at[second], y_recv.at[second]).wait()
        for b in (first, second):
            y_out[:, pl.ds(pl.multiple_of(b * LANES, LANES), LANES)] = ybuf[b, mine, :]
        both = jnp.concatenate([ybuf[first], ybuf[second]], axis=1)
        product = jnp.dot(left[...], three_right(both), preferred_element_type=F32)
        scores = []
        for side, b in enumerate((first, second)):
            at = pl.ds(pl.multiple_of(b * LANES, LANES), LANES)
            level = (2.0 / EPSILON * LOG2E) * (w[:, at] + product[:, side * LANES : (side + 1) * LANES])
            w[:, at] = level
            scores.append(level + gcol[pl.ds(b, 1), :])
        before = run_m[...]
        peak = jnp.maximum(before, jnp.maximum(scores[0], scores[1]))
        total = run_s[...] * jnp.exp2(before - peak)
        run_s[...] = total + jnp.exp2(scores[0] - peak) + jnp.exp2(scores[1] - peak)
        run_m[...] = peak

    own_block(0)

    def event(index, before):
        code = entry(index)
        dy, dz, half = parted(code)

        @pl.when(index < len(ORDER))
        def _():
            pass_on(dz, dy, half)

        @pl.when(index == 0)
        def _():
            own_block(1)
            drain(c1g, c1_sems.at[1])
            drain(w, z_sem)
            left[...] = three_left(c1g[...].reshape(PANEL, HEIGHT).T)

        @pl.when(index >= BEHIND)
        def _():
            take(before[-1])

        return (code, *before[:-1])

    lax.fori_loop(0, len(ORDER) + BEHIND, event, (jnp.int32(0),) * BEHIND)

    pltpu.make_async_copy(y_out, y_hbm, y_sem).start()

    def spread(line):
        return jnp.broadcast_to(line, (LANES, HEIGHT)).T

    def swap_cols(value, slot, buffer):
        sx[slot] = value
        buffer[q] = value
        other_cols(
            lambda col: remote(
                sx.at[slot], buffer.at[q], r_send.at[slot], r_recv.at[slot], r, col
            ).start()
        )
        rest = buffer.at[pl.ds(0, COLS - 1)]
        drain(rest, r_recv.at[slot])
        return buffer[...]

    m_t, s_t = run_m[...].T, run_s[...].T
    peak = jnp.max(m_t, axis=0, keepdims=True)
    line = peak + log2(jnp.sum(s_t * jnp.exp2(m_t - peak), axis=0, keepdims=True))
    lines = swap_cols(line, 0, rx1)
    peak = jnp.max(lines, axis=0)
    f1 = LOG2E * lr_ref[...] - peak - log2(jnp.sum(jnp.exp2(lines - peak[None]), axis=0))
    bcast[...] = spread(f1)

    def tile(b):
        return pl.ds(pl.multiple_of(b * LANES, LANES), LANES)

    def part_at(j):
        pair = j // 2
        dy = jnp.where(pair == 0, 2, jnp.where(pair == 1, 1, jnp.where(pair == 2, 3, 0)))
        return (yy + dy) % NY * 2 + (core + 1 + j) % 2

    def column_parts(work, source, slot, first):
        def one(j, carry):
            part = part_at(j)
            at = pl.ds(pl.multiple_of(part * 8, 8), 8)
            work(part * 8, at)

            @pl.when(j < GROUP - 1)
            def _():
                remote(
                    source.at[at, :], first.at[g], x_send.at[slot, 0], x_recv.at[slot, 0],
                    zh * GROUP + part, q,
                ).start()

            return carry

        lax.fori_loop(0, GROUP, one, 0)

    def over_strips(value, join):
        joined = [
            join(value(pl.ds(at, STRIP)).reshape(STRIP // 8, 8, LANES), axis=0)
            for at in range(0, HEIGHT, STRIP)
        ]
        return join(jnp.stack(joined), axis=0)

    def first_columns(b, at):
        tops, sums = [], []
        for k in range(8):
            cut = tile(b + k)
            tops.append(
                jnp.max(over_strips(lambda rows: w[rows, cut] + bcast[rows, :], jnp.max), axis=0, keepdims=True)
            )
        for k in range(8):
            cut = tile(b + k)

            def scaled(rows):
                value = jnp.exp2(w[rows, cut] + (bcast[rows, :] - tops[k]))
                w[rows, cut] = value
                return value

            sums.append(jnp.sum(over_strips(scaled, jnp.sum), axis=0, keepdims=True))
        top = jnp.concatenate(tops, axis=0)
        mloc[at, :] = top
        lcol[at, :] = top + log2(jnp.concatenate(sums, axis=0))

    column_parts(first_columns, lcol, 0, c1x)

    def join_rows(source, slot, first, second, third, join, p_recv):
        first[g] = source[pl.ds(pl.multiple_of(g * 8, 8), 8), :]
        drain(first.at[pl.ds(0, GROUP - 1)], x_recv.at[slot, 0])
        part = join(first[...])
        part1[slot] = part
        for dz in (2, 1, 3):
            remote(
                part1.at[slot], second.at[zh], x_send.at[slot, 1], x_recv.at[slot, 1],
                row_at(dz, 0, core), q,
            ).start()
        second[zh] = part
        drain(second.at[pl.ds(0, NZ - 1)], x_recv.at[slot, 1])
        whole = join(second[...])
        part2[slot] = whole

        def one(j, carry):
            row = zh * GROUP + part_at(j)
            remote(part2.at[slot], third.at[g], x_send.at[slot, 2], p_recv.at[g], row, q).start()
            return carry

        lax.fori_loop(0, GROUP - 1, one, 0)
        third[g] = whole

    def joined(parts):
        top = jnp.max(parts, axis=0)
        return top + log2(jnp.sum(jnp.exp2(parts - top[None]), axis=0))

    join_rows(lcol, 0, c1x, c2x, c3x, joined, p_recv)
    run_s[...] = jnp.zeros_like(run_s)

    def rows(step, carry):
        part = part_at(GROUP - 1 - step)

        @pl.when(step > 0)
        def _():
            drain(c3x.at[part], p_recv.at[part])

        at = pl.ds(pl.multiple_of(part * 8, 8), 8)
        level = LOG2E * lc_ref[at, :] - c3x[part]
        gcol[at, :] = level
        scale = jnp.exp2(level + mloc[at, :])
        u[at, :] = scale
        for top in range(0, HEIGHT, STRIP):
            strip = pl.ds(top, STRIP)
            total = run_s[strip, :]
            for k in range(8):
                total = total + w[strip, tile(part * 8 + k)] * scale[k : k + 1, :]
            run_s[strip, :] = total
        return carry

    lax.fori_loop(0, GROUP, rows, 0)
    line = jnp.sum(run_s[...].T, axis=0, keepdims=True)
    lines = swap_cols(line, 1, rx2)
    total = jnp.sum(lines, axis=0)
    f2 = LOG2E * lr_ref[...] + f1 - log2(total)
    row_out[...] = rc_ref[...] + EPSILON / LOG2E * f2
    bcast[...] = spread(jnp.exp(lr_ref[...]) / total)

    def second_columns(b, at):
        sums = [jnp.zeros((8, LANES), F32)] * 8
        for top in range(0, HEIGHT, STRIP):
            strip = pl.ds(top, STRIP)
            weight = bcast[strip, :]
            for k in range(8):
                product = w[strip, tile(b + k)] * weight
                sums[k] = sums[k] + jnp.sum(product.reshape(STRIP // 8, 8, LANES), axis=0)
        sums = [jnp.sum(value, axis=0, keepdims=True) for value in sums]
        lcol2[at, :] = jnp.concatenate(sums, axis=0) * u[at, :]

    column_parts(second_columns, lcol2, 1, d1x)
    join_rows(lcol2, 1, d1x, d2x, d3x, lambda parts: jnp.sum(parts, axis=0), q_recv)

    def result(step, carry):
        part = part_at(GROUP - 1 - step)

        @pl.when(step > 0)
        def _():
            drain(d3x.at[part], q_recv.at[part])

        at = pl.ds(pl.multiple_of(part * 8, 8), 8)
        level = LOG2E * lc_ref[at, :] + gcol[at, :] - log2(d3x[part])
        col_out[at, :] = cc_ref[at, :] + EPSILON / LOG2E * level
        return carry

    lax.fori_loop(0, GROUP, result, 0)

    drain(y_out, y_sem)
    drain(tslab.at[pl.ds(0, ROWS - 1)], t_sems.at[0])
    drain(c1g.at[pl.ds(0, COLS - 1)], c1_sems.at[0])
    drain(tall.at[pl.ds(0, COLS - 1)], tf_sems.at[0])
    for k in range(4):
        drain(c2c.at[0, pl.ds(0, ROWS - 1)], a_send.at[k])
    drain(ybuf.at[pl.ds(0, 12)], yp_send)
    drain(ybuf.at[pl.ds(0, 12)], ym_send)
    drain(ybuf.at[pl.ds(0, 6)], zz_send)
    drain(ybuf.at[pl.ds(0, 32)], core_send)
    for slot in range(2):
        drain(rx1.at[pl.ds(0, COLS - 1)], r_send.at[slot])
        drain(c1x.at[pl.ds(0, GROUP - 1)], x_send.at[slot, 0])
        drain(c2x.at[pl.ds(0, NZ - 1)], x_send.at[slot, 1])
        drain(c3x.at[pl.ds(0, GROUP - 1)], x_send.at[slot, 2])


def handed_on(*refs):
    for source, target in zip(refs[:3], refs[3:]):
        target[...] = source[...]


def body(y_prev, t_block, c2_panel, c1_panel, z_prev, row_const, col_const, log_row_mass, log_col_mass, col_warm):
    tall = lambda a: a.reshape(TILES, LANES)
    flat = lambda a: a.reshape(1, HEIGHT)
    hbm = pl.BlockSpec(memory_space=pl.ANY)
    vmem = pl.BlockSpec(memory_space=pltpu.VMEM)
    dma = pltpu.SemaphoreType.DMA
    y_next, row_pot, col_pot = pl.pallas_call(
        kernel,
        out_shape=(
            jax.ShapeDtypeStruct((DEPTH, WIDTH), F32),
            jax.ShapeDtypeStruct((1, HEIGHT), F32),
            jax.ShapeDtypeStruct((TILES, LANES), F32),
        ),
        in_specs=[hbm] * 10,
        out_specs=(hbm, vmem, vmem),
        scratch_shapes=[
            pltpu.VMEM((DEPTH, T_COLS), F32),
            pltpu.VMEM((1, HEIGHT), F32),
            pltpu.VMEM((TILES, LANES), F32),
            pltpu.VMEM((1, HEIGHT), F32),
            pltpu.VMEM((TILES, LANES), F32),
            pltpu.VMEM((TILES, LANES), F32),
            pltpu.VMEM((DEPTH, WIDTH), F32),
            dma((6,)),
            dma,
            pltpu.VMEM((HEIGHT, WIDTH), F32),
            pltpu.VMEM((TILES, PANEL, LANES), F32),
            pltpu.VMEM((2, ROWS, DEPTH, LANES), F32),
            pltpu.VMEM((2, ROWS, DEPTH, LANES), F32),
            pltpu.VMEM((1, PANEL), F32),
            pltpu.VMEM((ROWS, 1, PANEL), F32),
            pltpu.VMEM((COLS, ROWS, 1, PANEL), F32),
            pltpu.VMEM((PANEL // LANES, PANEL, LANES), F32),
            pltpu.VMEM((COLS, T_COLS, HEIGHT), F32),
            pltpu.VMEM((HEIGHT, 3 * PANEL), BF16),
            pltpu.VMEM((TILES, LANES), F32),
            pltpu.VMEM((HEIGHT, LANES), F32),
            pltpu.VMEM((HEIGHT, LANES), F32),
            pltpu.VMEM((HEIGHT, LANES), F32),
            pltpu.VMEM((2, 1, HEIGHT), F32),
            pltpu.VMEM((COLS, 1, HEIGHT), F32),
            pltpu.VMEM((COLS, 1, HEIGHT), F32),
            pltpu.VMEM((TILES, LANES), F32),
            pltpu.VMEM((TILES, LANES), F32),
            pltpu.VMEM((TILES, LANES), F32),
            pltpu.VMEM((2, 8, LANES), F32),
            pltpu.VMEM((2, 8, LANES), F32),
            pltpu.VMEM((TILES, LANES), F32),
            pltpu.VMEM((GROUP, 8, LANES), F32),
            pltpu.VMEM((NZ, 8, LANES), F32),
            pltpu.VMEM((GROUP, 8, LANES), F32),
            pltpu.VMEM((GROUP, 8, LANES), F32),
            pltpu.VMEM((NZ, 8, LANES), F32),
            pltpu.VMEM((GROUP, 8, LANES), F32),
            dma,
            dma((2,)),
            dma((2,)),
            dma((2,)),
            dma((4,)),
            dma((4,)),
            dma((TILES,)),
            dma,
            dma,
            dma,
            dma,
            dma((2,)),
            dma((2,)),
            dma((2, 3)),
            dma((2, 2)),
            dma((GROUP,)),
            dma((GROUP,)),
        ],
        compiler_params=pltpu.CompilerParams(
            collective_id=0, has_side_effects=True, vmem_limit_bytes=56 * 1024 * 1024
        ),
        name="step",
    )(
        y_prev, t_block, c2_panel, c1_panel.T, z_prev, flat(row_const), tall(col_const),
        flat(log_row_mass), tall(log_col_mass), tall(col_warm),
    )
    y_next, row_pot, col_pot = pl.pallas_call(
        handed_on,
        out_shape=(
            jax.ShapeDtypeStruct((DEPTH, WIDTH), F32),
            jax.ShapeDtypeStruct((1, HEIGHT), F32),
            jax.ShapeDtypeStruct((TILES, LANES), F32),
        ),
        in_specs=[vmem] * 3,
        out_specs=(vmem, vmem, vmem),
        name="results",
    )(y_next, row_pot, col_pot)
    return y_next, row_pot.reshape(HEIGHT), col_pot.reshape(WIDTH)


def solution(mesh):
    block = P("row", "col")
    return jax.shard_map(
        body,
        mesh=mesh,
        in_specs=(block,) * 5 + (P("row"), P("col"), P("row"), P("col"), P("col")),
        out_specs=(block, P("row"), P("col")),
        check_vma=False,
    )
```
